32 devices in a mesh: seq: 4 (over y, x), head: 8 (over z, core).
Axes of the slice: x: 2, y: 2, z: 4, core: 2. Of those that a mesh axis runs over, the one named last changes fastest.
Arguments:
- inputs: bfloat16 [6144, 2048], P(('seq', 'head')), may hold values from -6 to 6
- segments: int32 [4, 1536], P('seq'), may hold values from 0 to 3, never falling along the last dimension, each value on 1 to 1024 neighbouring positions
- cotangent: bfloat16 [6144, 2048], P(('seq', 'head')), may hold values from -6 to 6
- norm_attn: bfloat16 [2048], P(('seq', 'head')), may hold values from 0.099609375 to 1.8984375
- attn_in: bfloat16 [2048, 1536], P(('seq', 'head')), may hold values from -0.125 to 0.125
- norm_latent: bfloat16 [1024], P(('seq', 'head')), may hold values from 0.099609375 to 1.8984375
- query_up: bfloat16 [1024, 4096], P(None, 'head'), may hold values from -0.1875 to 0.1875
- out_proj: bfloat16 [4096, 2048], P('head'), may hold values from -0.375 to 0.375
- norm_mlp: bfloat16 [2048], P(('seq', 'head')), may hold values from 0.099609375 to 1.8984375
- gate_up: bfloat16 [2048, 11264], P(('seq', 'head')), may hold values from -0.125 to 0.125
- down_proj: bfloat16 [5632, 2048], P(('seq', 'head')), may hold values from -0.078125 to 0.078125
Outputs:
- layer_out: bfloat16 [6144, 2048], P(('seq', 'head'))
- input_grad: float32 [6144, 2048], P(('seq', 'head'))
- attnnorm_grad: float32 [2048], P(('seq', 'head'))
- attnin_grad: float32 [2048, 1536], P(('seq', 'head'))
- latnorm_grad: float32 [1024], P(('seq', 'head'))
- queryup_grad: float32 [1024, 4096], P('seq', 'head')
- outproj_grad: float32 [4096, 2048], P('head', 'seq')
- mlpnorm_grad: float32 [2048], P(('seq', 'head'))
- gateup_grad: float32 [2048, 11264], P(('seq', 'head'))
- downproj_grad: float32 [5632, 2048], P(('seq', 'head'))
The draws below stay inside these ranges and needn't reach their ends.
Inputs may be any that keep to these rules, and one draw needn't show every extreme that they name: `segments`: in each packed row the ids never fall, every id occurs, and each document holds at most 1024 tokens.
All inputs are finite; a program needn't handle non-finite values.
Results may differ from the reference program's by a relative error of at most 0.018.
Values may be sent and summed in bfloat16 or wider, within the bound.
A program may use at most 320 MiB of HBM per device.

```python
import math
import jax
import jax.numpy as jnp
import numpy as np
from jax import lax

D = 2048
H = 16
DH = 256
QR = 1024
FF = 5632
SEG_COUNT = 4
TOK_GRP = 1536
TOKENS = 6144
SEG_MOST = 1024
N_SEQ = 4


def block_levels(stream_key, extent, cuts, low, largest):
    gain = 1.0
    for position, shards_of in cuts:
        heights = jax.random.uniform(jax.random.fold_in(jax.random.fold_in(stream_key, 6), position), (shards_of,), jnp.float32, low / len(cuts), largest / len(cuts))
        gain = gain * jnp.repeat(jnp.exp(heights), extent[position] // shards_of).reshape((-1,) + (1,) * (len(extent) - 1 - position))
    return gain


def length_profile(amount, total, most, lean):
    loads = [(1 << 20) // math.isqrt(grade ** lean) + 1 for grade in range(2, amount + 1)]
    spare, given = total - most - (amount - 1), [1] * (amount - 1)
    while spare > 0:
        candidates = [i for i in range(amount - 1) if given[i] < most]
        whole, budget = sum([loads[i] for i in candidates]), spare
        for i in candidates:
            extra = min(most - given[i], max(1, budget * loads[i] // whole), spare)
            given[i] = given[i] + extra
            spare = spare - extra
    return np.array([most] + given)


def uneven(own_key, count, total, reach, skew):
    if count == 2:
        one = jax.random.randint(own_key, (), max(1, total - reach), min(reach, total - 1) + 1)
        return jnp.stack([one, total - one])
    sizes = jnp.asarray(length_profile(count, total, reach, skew), jnp.int32)
    pairs = (count - 1) // 2
    donor, taker = sizes[1:1 + 2 * pairs:2], sizes[2:2 + 2 * pairs:2]
    margin = jnp.minimum(donor - 1, reach - taker)
    shifted = jax.random.randint(jax.random.fold_in(own_key, 1), (pairs,), 0, 1 << 20) % (margin + 1)
    sizes = sizes.at[1:1 + 2 * pairs:2].set(donor - shifted).at[2:2 + 2 * pairs:2].set(taker + shifted)
    return sizes[jax.random.permutation(jax.random.fold_in(own_key, 2), count)]


def noise(rng, shape, width, reach, cuts=(), kind=jnp.bfloat16):
    result = width * jax.random.normal(rng, shape, jnp.float32)
    if cuts:
        result = result * block_levels(rng, shape, cuts, -0.22, 0.18)
    return jnp.clip(result, -reach, reach).astype(kind)


def setup_inputs(seed: int = 0) -> dict:
    seeds = jax.random.split(jax.random.key(seed), 12)
    inputs = noise(seeds[0], (TOKENS, D), 1.0, 6.0, ((0, 32),))
    segments = jax.vmap(lambda own: jnp.searchsorted(jnp.cumsum(uneven(own, SEG_COUNT, TOK_GRP, SEG_MOST, 1)), jnp.arange(TOK_GRP), side="right"))(jax.random.split(seeds[1], N_SEQ)).reshape((N_SEQ, TOK_GRP)).astype(jnp.int32)
    cotangent = noise(seeds[2], (TOKENS, D), 1.0, 6.0, ((0, 32),))
    norm_attn = jnp.clip(1.0 + 0.18 * jax.random.normal(seeds[3], (D,), jnp.float32), 0.099609375, 1.8984375).astype(jnp.bfloat16)
    attn_in = noise(seeds[4], (D, QR + 2 * DH), D ** -0.5, 0.125, ((0, 32),))
    norm_latent = jnp.clip(1.0 + 0.18 * jax.random.normal(seeds[5], (QR,), jnp.float32), 0.099609375, 1.8984375).astype(jnp.bfloat16)
    query_up = noise(seeds[6], (QR, H * DH), QR ** -0.5, 0.1875, ((1, 8),))
    out_proj = noise(seeds[7], (H * DH, D), (H * DH // 16) ** -0.5, 0.375, ((0, 8),))
    norm_mlp = jnp.clip(1.0 + 0.18 * jax.random.normal(seeds[8], (D,), jnp.float32), 0.099609375, 1.8984375).astype(jnp.bfloat16)
    gate_up = noise(seeds[9], (D, 2 * FF), D ** -0.5, 0.125, ((0, 32),))
    down_proj = noise(seeds[10], (FF, D), FF ** -0.5, 0.078125, ((0, 32),))
    return {"inputs": inputs, "segments": segments, "cotangent": cotangent, "norm_attn": norm_attn, "attn_in": attn_in, "norm_latent": norm_latent, "query_up": query_up, "out_proj": out_proj, "norm_mlp": norm_mlp, "gate_up": gate_up, "down_proj": down_proj}


@jax.custom_vjp
def low(v):
    return lax.optimization_barrier(v.astype(jnp.bfloat16)).astype(jnp.float32)

@jax.custom_vjp
def low_back(v):
    return v

def low_keep(v):
    return (low(v), None)

def low_pass(kept, grad):
    return (grad,)

def back_keep(v):
    return (v, None)

def back_low(kept, grad):
    return (low(grad),)
low.defvjp(low_keep, low_pass)
low_back.defvjp(back_keep, back_low)
EPS = 1e-06
THETA = 10000.0
NEG = -1e+30

def product(left, right):
    return jnp.dot(left, right, precision=lax.Precision.HIGHEST, preferred_element_type=jnp.float32)

def rms_norm(values_in, gain_vec):
    return values_in * lax.rsqrt(lax.optimization_barrier(jnp.mean(values_in * values_in, axis=-1, keepdims=True)) + EPS) * gain_vec

def rotary(values_in, cosine, sine):
    half_dim = values_in.shape[-1] // 2
    first_half = values_in[..., :half_dim]
    second_half = values_in[..., half_dim:]
    return jnp.concatenate([first_half * cosine - second_half * sine, second_half * cosine + first_half * sine], axis=-1)

def segment_starts(segment_row):
    index = jnp.arange(segment_row.shape[0], dtype=jnp.int32)
    opens = jnp.concatenate([jnp.ones((1,), jnp.bool_), segment_row[1:] != segment_row[:-1]])
    return lax.cummax(jnp.where(opens, index, jnp.zeros_like(index)), axis=0)

def angles(segment_row):
    index = jnp.arange(segment_row.shape[0], dtype=jnp.int32)
    places = (index - segment_starts(segment_row)).astype(jnp.float32)
    exponent = jnp.arange(DH // 2, dtype=jnp.float32) * (-2.0 / DH)
    frequency = jnp.power(jnp.float32(THETA), exponent)
    turned = places[:, None] * frequency[None, :]
    return (jnp.cos(turned), jnp.sin(turned))

def row_forward(params, row_in, segment_row):
    norm_attn, attn_in, norm_latent, query_up, out_proj, norm_mlp, gate_up, down_proj = params
    length = row_in.shape[0]
    cosine, sine = angles(segment_row)
    normed = low(rms_norm(row_in, norm_attn))
    projected = product(normed, attn_in)
    latent = low_back(projected[:, :QR])
    key_raw = low_back(projected[:, QR:QR + DH])
    values = low_back(low(projected[:, QR + DH:]))
    latent_n = low(rms_norm(latent, norm_latent))
    keys = low(rotary(key_raw, cosine, sine))
    query_raw = low_back(product(latent_n, query_up))
    queries = low(rotary(query_raw.reshape(length, H, DH), cosine[:, None, :], sine[:, None, :]))
    score_scale = DH ** (-0.5)
    query_rows = min(512, length)
    index = jnp.arange(length, dtype=jnp.int32)

    def attend(row_start):
        query_blk = lax.dynamic_slice_in_dim(queries, row_start, query_rows, 0)
        seg_query = lax.dynamic_slice_in_dim(segment_row, row_start, query_rows, 0)
        place_query = row_start + jnp.arange(query_rows, dtype=jnp.int32)
        raw = jnp.einsum('qhd,kd->hqk', query_blk, keys, precision=lax.Precision.HIGHEST)
        allowed = (seg_query[:, None] == segment_row[None, :]) & (place_query[:, None] >= index[None, :])
        scores = low_back(jnp.where(allowed[None], raw * score_scale, NEG))
        attention = jax.nn.softmax(scores, axis=-1)
        return jnp.einsum('hqk,kd->qhd', low(attention), values, precision=lax.Precision.HIGHEST)
    starts = jnp.arange(length // query_rows, dtype=jnp.int32) * query_rows
    blocks = lax.map(jax.checkpoint(attend), starts)
    mixed = low_back(low(blocks.reshape(length, H * DH)))
    attn_out = low_back(product(mixed, out_proj))
    hidden = row_in + attn_out
    normed_mlp = low(rms_norm(hidden, norm_mlp))
    joined = product(normed_mlp, gate_up)
    gate_part = low_back(joined[:, :FF])
    up_part = low_back(joined[:, FF:])
    activated = low(jax.nn.silu(gate_part) * up_part)
    return hidden + product(activated, down_proj)

def reference(inputs, segments, cotangent, norm_attn, attn_in, norm_latent, query_up, out_proj, norm_mlp, gate_up, down_proj):
    params = tuple((weight.astype(jnp.float32) for weight in (norm_attn, attn_in, norm_latent, query_up, out_proj, norm_mlp, gate_up, down_proj)))
    row_count = segments.shape[0]
    length = segments.shape[1]
    rows_in = inputs.astype(jnp.float32).reshape(row_count, length, D)
    rows_grad = cotangent.astype(jnp.float32).reshape(row_count, length, D)

    def one_row(totals, pieces):
        row_in, row_grad, segment_row = pieces
        row_out, pullback = jax.vjp(lambda weights, values_in: row_forward(weights, values_in, segment_row), params, row_in)
        weight_grads, input_grad = pullback(row_grad)
        return (jax.tree.map(jnp.add, totals, weight_grads), (row_out, input_grad))
    zeros = jax.tree.map(jnp.zeros_like, params)
    totals, (outputs, input_grads) = lax.scan(one_row, zeros, (rows_in, rows_grad, segments))
    return (outputs.reshape(row_count * length, D).astype(jnp.bfloat16), input_grads.reshape(row_count * length, D), totals[0], totals[1], totals[2], totals[3], totals[4], totals[5], totals[6], totals[7])
```

```python
import jax
import jax.numpy as jnp
from jax import lax
from jax.sharding import PartitionSpec as P

DH = 256
QR = 1024
FF = 5632


EPS = 1e-06
THETA = 10000.0
NEG = -1e30


def contract(left, right):
    return lax.dot_general(
        left, right, (((1,), (1,)), ((), ())), preferred_element_type=jnp.float32
    )


def transposed(left, right):
    return lax.dot_general(
        left, right, (((0,), (0,)), ((), ())), preferred_element_type=jnp.float32
    )


def rms_norm(values_in, gain_vec):
    return (
        values_in
        * lax.rsqrt(jnp.mean(values_in * values_in, axis=-1, keepdims=True) + EPS)
        * gain_vec
    )


def rotary(values_in, cosine, sine):
    half_dim = values_in.shape[-1] // 2
    first_half = values_in[..., :half_dim]
    second_half = values_in[..., half_dim:]
    return jnp.concatenate(
        [first_half * cosine - second_half * sine, second_half * cosine + first_half * sine],
        axis=-1,
    )


def segment_starts(segment_row):
    index = jnp.arange(segment_row.shape[0], dtype=jnp.int32)
    opens = jnp.concatenate([jnp.ones((1,), jnp.bool_), segment_row[1:] != segment_row[:-1]])
    return lax.cummax(jnp.where(opens, index, jnp.zeros_like(index)), axis=0)


def angles(segment_row):
    index = jnp.arange(segment_row.shape[0], dtype=jnp.int32)
    places = (index - segment_starts(segment_row)).astype(jnp.float32)
    exponent = jnp.arange(DH // 2, dtype=jnp.float32) * (-2.0 / DH)
    frequency = jnp.power(jnp.float32(THETA), exponent)
    turned = places[:, None] * frequency[None, :]
    return (jnp.cos(turned), jnp.sin(turned))


def shards(
    inputs,
    segments,
    cotangent,
    norm_attn,
    attn_in,
    norm_latent,
    query_up,
    out_proj,
    norm_mlp,
    gate_up,
    down_proj,
):
    head_count = lax.axis_size("head")
    head_place = lax.axis_index("head")
    shard_rows = inputs.shape[0]
    group_rows = shard_rows * head_count
    heads_dev = query_up.shape[1] // DH
    block_rows = min(512, group_rows)
    block_count = group_rows // block_rows
    score_scale = DH ** (-0.5)
    seq_count = lax.axis_size("seq")
    own_rows = attn_in.shape[0]
    own_latent = norm_latent.shape[0]
    own_units = down_proj.shape[0]
    units = seq_count * own_units
    device_count = seq_count * head_count
    proj_cols = attn_in.shape[1]
    gain_cols = jnp.stack(
        [norm_attn, norm_mlp, jnp.pad(norm_latent, (0, own_rows - own_latent))], axis=1
    )
    packed = jnp.concatenate([attn_in, jnp.pad(gain_cols, ((0, 0), (0, 125)))], axis=1)
    packed_all = lax.all_gather(packed, ("seq", "head"), axis=0, tiled=True)
    weight_in = packed_all[:, :proj_cols]
    gain_attn = packed_all[:, proj_cols].astype(jnp.float32)
    gain_mlp = packed_all[:, proj_cols + 1].astype(jnp.float32)
    gain_latent = (
        packed_all[:, proj_cols + 2]
        .reshape(device_count, own_rows)[:, :own_latent]
        .reshape(device_count * own_latent)
        .astype(jnp.float32)
    )
    pieces = gate_up.reshape(own_rows, 2, seq_count, head_count, own_units)
    pieces = pieces.transpose(3, 0, 1, 2, 4).reshape(head_count, own_rows, 2 * units)
    turned = lax.all_to_all(pieces, "head", split_axis=0, concat_axis=0, tiled=True)
    weight_gu = lax.all_gather(
        turned.reshape(head_count * own_rows, 2 * units), "seq", axis=0, tiled=True
    )
    weight_gate = weight_gu[:, :units]
    weight_up = weight_gu[:, units:]
    weight_down = lax.all_gather(down_proj, "seq", axis=0, tiled=True)
    cot_all = lax.all_gather(cotangent, "head", axis=0, tiled=True)
    segment_row = segments[0]
    cosine, sine = angles(segment_row)
    row_start = head_place * shard_rows
    cos_local = lax.dynamic_slice_in_dim(cosine, row_start, shard_rows, 0)
    sin_local = lax.dynamic_slice_in_dim(sine, row_start, shard_rows, 0)
    inputs_f = inputs.astype(jnp.float32)
    normed = rms_norm(inputs_f, gain_attn).astype(jnp.bfloat16)
    projected = jnp.dot(normed, weight_in, preferred_element_type=jnp.float32)
    latent = projected[:, :QR]
    key_raw = projected[:, QR : QR + DH]
    latent_n = rms_norm(latent, gain_latent).astype(jnp.bfloat16)
    keys_local = rotary(key_raw, cos_local, sin_local).astype(jnp.bfloat16)
    values_local = projected[:, QR + DH :].astype(jnp.bfloat16)
    joined_all = lax.all_gather(
        jnp.concatenate([latent_n, keys_local, values_local], axis=1), "head", axis=0, tiled=True
    )
    latent_all, keys, values = (
        joined_all[:, :QR],
        joined_all[:, QR : QR + DH],
        joined_all[:, QR + DH :],
    )
    query_raw = jnp.dot(latent_all, query_up, preferred_element_type=jnp.float32)
    queries = rotary(
        query_raw.reshape(group_rows, heads_dev, DH), cosine[:, None, :], sine[:, None, :]
    ).astype(jnp.bfloat16)

    def lowest():
        return jnp.zeros((), jnp.int32)

    def query_block(source, qblock):
        piece = lax.dynamic_slice_in_dim(source, qblock * block_rows, block_rows, 0)
        return piece.reshape(block_rows * heads_dev, DH)

    def scores_of(query_blk, qblock, kblock):
        key_blk = lax.dynamic_slice_in_dim(keys, kblock * block_rows, block_rows, 0)
        raw = contract(query_blk, key_blk).reshape(block_rows, heads_dev, block_rows) * score_scale
        place_query = qblock * block_rows + jnp.arange(block_rows, dtype=jnp.int32)
        place_key = kblock * block_rows + jnp.arange(block_rows, dtype=jnp.int32)
        seg_query = lax.dynamic_slice_in_dim(segment_row, qblock * block_rows, block_rows, 0)
        seg_key = lax.dynamic_slice_in_dim(segment_row, kblock * block_rows, block_rows, 0)
        allowed = (seg_query[:, None] == seg_key[None, :]) & (
            place_query[:, None] >= place_key[None, :]
        )
        return jnp.where(allowed[:, None, :], raw, NEG)

    def forward_block(qblock):
        query_blk = query_block(queries, qblock)
        first_key = lowest()

        def max_step(kblock, state):
            row_top, row_total = state
            scores = scores_of(query_blk, qblock, kblock)
            new_top = jnp.maximum(row_top, jnp.max(scores, axis=-1))
            row_total = row_total * jnp.exp(row_top - new_top) + jnp.sum(
                jnp.exp(scores - new_top[..., None]), axis=-1
            )
            return (new_top, row_total)

        start_state = (
            jnp.full((block_rows, heads_dev), NEG, jnp.float32),
            jnp.zeros((block_rows, heads_dev), jnp.float32),
        )
        row_top, row_total = lax.fori_loop(first_key, qblock + 1, max_step, start_state)

        def value_step(kblock, accum):
            scores = scores_of(query_blk, qblock, kblock)
            attention = jnp.exp(scores - row_top[..., None]) / row_total[..., None]
            value_blk = lax.dynamic_slice_in_dim(values, kblock * block_rows, block_rows, 0)
            weights_b = attention.astype(jnp.bfloat16).reshape(block_rows * heads_dev, block_rows)
            return accum + jnp.dot(weights_b, value_blk, preferred_element_type=jnp.float32)

        accum = lax.fori_loop(
            first_key, qblock + 1, value_step, jnp.zeros((block_rows * heads_dev, DH), jnp.float32)
        )
        return (accum.astype(jnp.bfloat16).reshape(block_rows, heads_dev * DH), row_top, row_total)

    block_ids = jnp.arange(block_count, dtype=jnp.int32)
    mixed_blocks, row_tops, row_totals = lax.map(forward_block, block_ids)
    mixed = mixed_blocks.reshape(group_rows, heads_dev * DH)
    piece = mixed
    attn_out = lax.psum_scatter(
        jnp.dot(piece, out_proj, preferred_element_type=jnp.float32).astype(jnp.bfloat16),
        "head",
        scatter_dimension=0,
        tiled=True,
    ).astype(jnp.float32)
    hidden = inputs_f + attn_out
    normed_mlp = rms_norm(hidden, gain_mlp).astype(jnp.bfloat16)
    nmlp_all = lax.all_gather(normed_mlp, "head", axis=0, tiled=True)
    gate_part = jnp.dot(nmlp_all, weight_gate, preferred_element_type=jnp.float32)
    up_part = jnp.dot(nmlp_all, weight_up, preferred_element_type=jnp.float32)
    activated = (jax.nn.silu(gate_part) * up_part).astype(jnp.bfloat16)
    down_part = jnp.dot(activated, weight_down, preferred_element_type=jnp.float32)
    grad_act = contract(cot_all, weight_down)
    silu_prod, act_back = jax.vjp(
        lambda gate_in, up_in: jax.nn.silu(gate_in) * up_in, gate_part, up_part
    )
    grad_gate, grad_up = act_back(grad_act)
    grad_gate = grad_gate.astype(jnp.bfloat16)
    grad_up = grad_up.astype(jnp.bfloat16)
    grad_nmlp = lax.psum_scatter(
        (contract(grad_gate, weight_gate) + contract(grad_up, weight_up)).astype(jnp.bfloat16),
        "head",
        scatter_dimension=0,
        tiled=True,
    ).astype(jnp.float32)
    down_out = lax.psum_scatter(
        down_part.astype(jnp.bfloat16), "head", scatter_dimension=0, tiled=True
    ).astype(jnp.float32)
    layer_out = (hidden + down_out).astype(jnp.bfloat16)
    down_grad = transposed(activated, cot_all).astype(jnp.bfloat16)
    gu_grad = jnp.concatenate(
        [
            transposed(nmlp_all, grad_gate).astype(jnp.bfloat16),
            transposed(nmlp_all, grad_up).astype(jnp.bfloat16),
        ],
        axis=1,
    )
    downproj_grad = lax.psum_scatter(
        down_grad, "seq", scatter_dimension=0, tiled=True
    ).astype(jnp.float32)
    gu_rows = lax.psum_scatter(gu_grad, "seq", scatter_dimension=0, tiled=True)
    gu_back = lax.all_to_all(
        gu_rows.reshape(head_count, own_rows, 2 * units),
        "head",
        split_axis=0,
        concat_axis=0,
        tiled=True,
    )
    gateup_grad = (
        gu_back.reshape(head_count, own_rows, 2, seq_count, own_units)
        .transpose(1, 2, 3, 0, 4)
        .reshape(own_rows, 2 * device_count * own_units)
        .astype(jnp.float32)
    )
    norm_value, mlp_back = jax.vjp(rms_norm, hidden, gain_mlp)
    grad_hidden_n, mlpnorm_part = mlp_back(grad_nmlp)
    grad_hidden = cotangent.astype(jnp.float32) + grad_hidden_n
    grad_attn = grad_hidden.astype(jnp.bfloat16)
    grad_attn_all = lax.all_gather(grad_attn, "head", axis=0, tiled=True)
    grad_mixed = contract(grad_attn_all, out_proj).astype(jnp.bfloat16)
    outproj_local = transposed(grad_attn_all, mixed)

    def back_block(state, qblock):
        key_accum, value_accum = state
        query_blk = query_block(queries, qblock)
        grad_out = query_block(grad_mixed, qblock)
        row_top = row_tops[qblock]
        row_total = row_totals[qblock]
        first_key = lowest()

        def weights_and_grads(kblock):
            scores = scores_of(query_blk, qblock, kblock)
            attention = jnp.exp(scores - row_top[..., None]) / row_total[..., None]
            value_blk = lax.dynamic_slice_in_dim(values, kblock * block_rows, block_rows, 0)
            grad_weights = contract(grad_out, value_blk).reshape(block_rows, heads_dev, block_rows)
            return (attention, grad_weights)

        def dots_step(kblock, row_dots):
            attention, grad_weights = weights_and_grads(kblock)
            return row_dots + jnp.sum(attention * grad_weights, axis=-1)

        row_dots = lax.fori_loop(
            first_key, qblock + 1, dots_step, jnp.zeros((block_rows, heads_dev), jnp.float32)
        )

        def grad_step(kblock, inner_state):
            query_grad, key_acc, value_acc = inner_state
            attention, grad_weights = weights_and_grads(kblock)
            grad_scores = (
                (attention * (grad_weights - row_dots[..., None]))
                .astype(jnp.bfloat16)
                .reshape(block_rows * heads_dev, block_rows)
            )
            key_blk = lax.dynamic_slice_in_dim(keys, kblock * block_rows, block_rows, 0)
            query_grad = (
                query_grad
                + jnp.dot(grad_scores, key_blk, preferred_element_type=jnp.float32) * score_scale
            )
            key_part = transposed(grad_scores, query_blk) * score_scale
            weights_b = attention.astype(jnp.bfloat16).reshape(block_rows * heads_dev, block_rows)
            value_part = transposed(weights_b, grad_out)
            key_old = lax.dynamic_slice_in_dim(key_acc, kblock * block_rows, block_rows, 0)
            value_old = lax.dynamic_slice_in_dim(value_acc, kblock * block_rows, block_rows, 0)
            key_acc = lax.dynamic_update_slice_in_dim(
                key_acc, key_old + key_part, kblock * block_rows, 0
            )
            value_acc = lax.dynamic_update_slice_in_dim(
                value_acc, value_old + value_part, kblock * block_rows, 0
            )
            return (query_grad, key_acc, value_acc)

        start_inner = (jnp.zeros((block_rows * heads_dev, DH), jnp.float32), key_accum, value_accum)
        query_grad, key_accum, value_accum = lax.fori_loop(
            first_key, qblock + 1, grad_step, start_inner
        )
        return ((key_accum, value_accum), query_grad)

    start_outer = (
        jnp.zeros((group_rows, DH), jnp.float32),
        jnp.zeros((group_rows, DH), jnp.float32),
    )
    (key_grads, value_grads), query_grads = lax.scan(back_block, start_outer, block_ids)
    query_grads = query_grads.reshape(group_rows, heads_dev, DH)
    turned_query, query_back = jax.vjp(
        lambda query_in: rotary(query_in, cosine[:, None, :], sine[:, None, :]),
        query_raw.reshape(group_rows, heads_dev, DH),
    )
    (grad_query,) = query_back(query_grads)
    grad_query = grad_query.reshape(group_rows, heads_dev * DH).astype(jnp.bfloat16)
    queryup_local = transposed(latent_all, grad_query)
    grad_latent_part = contract(grad_query, query_up)
    received = lax.psum_scatter(
        jnp.concatenate([grad_latent_part, key_grads, value_grads], axis=1).astype(jnp.bfloat16),
        "head",
        scatter_dimension=0,
        tiled=True,
    ).astype(jnp.float32)
    grad_latent_n, grad_keys, grad_values = (
        received[:, :QR],
        received[:, QR : QR + DH],
        received[:, QR + DH :],
    )
    queryup_grad, outproj_turned = (
        lax.psum_scatter(
            queryup_local.astype(jnp.bfloat16), "seq", scatter_dimension=0, tiled=True
        ).astype(jnp.float32),
        lax.psum_scatter(
            outproj_local.astype(jnp.bfloat16), "seq", scatter_dimension=0, tiled=True
        ).astype(jnp.float32),
    )
    outproj_grad = outproj_turned.T
    latent_value, latent_back = jax.vjp(rms_norm, latent, gain_latent)
    grad_latent, latnorm_part = latent_back(grad_latent_n)
    turned_key, key_back = jax.vjp(lambda key_in: rotary(key_in, cos_local, sin_local), key_raw)
    (grad_key_raw,) = key_back(grad_keys)
    grad_proj = jnp.concatenate([grad_latent, grad_key_raw, grad_values], axis=1).astype(
        jnp.bfloat16
    )
    attnin_part = transposed(normed, grad_proj)
    grad_normed = contract(grad_proj, weight_in)
    input_value, input_back = jax.vjp(rms_norm, inputs_f, gain_attn)
    grad_input_n, attnnorm_part = input_back(grad_normed)
    input_grad = grad_hidden + grad_input_n
    latent_col = jnp.pad(
        latnorm_part.reshape(device_count, own_latent), ((0, 0), (0, own_rows - own_latent))
    ).reshape(device_count * own_rows)
    gain_parts = jnp.stack([attnnorm_part, mlpnorm_part, latent_col], axis=1)
    packed_part = jnp.concatenate(
        [attnin_part, jnp.pad(gain_parts, ((0, 0), (0, 125)))], axis=1
    ).astype(jnp.bfloat16)
    packed_grad = lax.psum_scatter(
        packed_part, ("seq", "head"), scatter_dimension=0, tiled=True
    ).astype(jnp.float32)
    attnin_grad = packed_grad[:, :proj_cols]
    attnnorm_grad = packed_grad[:, proj_cols]
    mlpnorm_grad = packed_grad[:, proj_cols + 1]
    latnorm_grad = packed_grad[:own_latent, proj_cols + 2]
    return (
        layer_out,
        input_grad,
        attnnorm_grad,
        attnin_grad,
        latnorm_grad,
        queryup_grad,
        outproj_grad,
        mlpnorm_grad,
        gateup_grad,
        downproj_grad,
    )


def solution(mesh):
    in_specs = (
        P(("seq", "head"), None),
        P("seq", None),
        P(("seq", "head"), None),
        P(("seq", "head")),
        P(("seq", "head"), None),
        P(("seq", "head")),
        P(None, "head"),
        P("head", None),
        P(("seq", "head")),
        P(("seq", "head"), None),
        P(("seq", "head"), None),
    )
    out_specs = (
        P(("seq", "head"), None),
        P(("seq", "head"), None),
        P(("seq", "head")),
        P(("seq", "head"), None),
        P(("seq", "head")),
        P("seq", "head"),
        P("head", "seq"),
        P(("seq", "head")),
        P(("seq", "head"), None),
        P(("seq", "head"), None),
    )
    return jax.shard_map(shards, mesh=mesh, in_specs=in_specs, out_specs=out_specs, check_vma=False)
```

```python
import functools

import jax
import jax.numpy as jnp
from jax import lax
from jax.experimental import pallas as pl
from jax.experimental.pallas import tpu as pltpu
from jax.sharding import PartitionSpec as P

DH = 256
QR = 1024
HALF = DH // 2


EPS = 1e-06
THETA = 10000.0
NEG = -1e30


def contract(left, right):
    return lax.dot_general(
        left, right, (((1,), (1,)), ((), ())), preferred_element_type=jnp.float32
    )


def transposed(left, right):
    return lax.dot_general(
        left, right, (((0,), (0,)), ((), ())), preferred_element_type=jnp.float32
    )


def matmul(left, right):
    return jnp.dot(left, right, preferred_element_type=jnp.float32)


def rms_norm(values_in, gain_vec):
    return (
        values_in
        * lax.rsqrt(jnp.mean(values_in * values_in, axis=-1, keepdims=True) + EPS)
        * gain_vec
    )


def rotary(values_in, cosine, sine):
    half_dim = values_in.shape[-1] // 2
    first_half = values_in[..., :half_dim]
    second_half = values_in[..., half_dim:]
    return jnp.concatenate(
        [first_half * cosine - second_half * sine, second_half * cosine + first_half * sine],
        axis=-1,
    )


def segment_starts(segment_row):
    index = jnp.arange(segment_row.shape[0], dtype=jnp.int32)
    opens = jnp.concatenate([jnp.ones((1,), jnp.bool_), segment_row[1:] != segment_row[:-1]])
    return lax.cummax(jnp.where(opens, index, jnp.zeros_like(index)), axis=0)


def angles(starts):
    index = jnp.arange(starts.shape[0], dtype=jnp.int32)
    places = (index - starts).astype(jnp.float32)
    exponent = jnp.arange(DH // 2, dtype=jnp.float32) * (-2.0 / DH)
    frequency = jnp.power(jnp.float32(THETA), exponent)
    turned = places[:, None] * frequency[None, :]
    return (jnp.cos(turned), jnp.sin(turned))


def stacked(values_in, heads):
    return jnp.concatenate([values_in[:, h * DH : (h + 1) * DH] for h in range(heads)], axis=0)


def side_by_side(values_in, heads):
    rows = values_in.shape[0] // heads
    return jnp.concatenate([values_in[h * rows : (h + 1) * rows] for h in range(heads)], axis=1)


def block_mask(starts, query_row, key_row, heads, rows, cols):
    place_query = query_row + lax.broadcasted_iota(jnp.int32, (rows, cols), 0)
    place_key = key_row + lax.broadcasted_iota(jnp.int32, (rows, cols), 1)
    allowed = (place_key >= starts) & (place_key <= place_query)
    return jnp.concatenate([allowed] * heads, axis=0) if heads > 1 else allowed


def forward_kernel(
    heads,
    block,
    first_ref,
    joined_ref,
    starts_ref,
    cos_ref,
    sin_ref,
    queryup_ref,
    outproj_ref,
    part_ref,
    query_ref,
    mixed_ref,
    stats_ref,
    top_ref,
    total_ref,
    accum_ref,
):
    qblock = pl.program_id(0)
    query_row = pl.multiple_of(qblock * block, block)
    cosine = cos_ref[...]
    sine = sin_ref[...]
    raw = matmul(joined_ref[pl.ds(query_row, block), :QR], queryup_ref[...])
    turned = []
    for h in range(heads):
        one = raw[:, h * DH : h * DH + HALF]
        two = raw[:, h * DH + HALF : (h + 1) * DH]
        turned += [one * cosine - two * sine, two * cosine + one * sine]
    queries = (jnp.concatenate(turned, axis=1)).astype(jnp.bfloat16) * jnp.bfloat16(DH**-0.5)
    query_ref[...] = queries
    rows = stacked(queries, heads)
    starts = starts_ref[...]
    top_ref[...] = jnp.full_like(top_ref, NEG)
    total_ref[...] = jnp.zeros_like(total_ref)
    accum_ref[...] = jnp.zeros_like(accum_ref)

    def key_step(kblock, carry):
        key_row = pl.multiple_of(kblock * block, block)
        keys = joined_ref[pl.ds(key_row, block), QR : QR + DH]
        values = joined_ref[pl.ds(key_row, block), QR + DH :]
        scores = contract(rows, keys)
        allowed = block_mask(starts, query_row, key_row, heads, block, block)
        scores = jnp.where(allowed, scores, NEG)
        old_top = top_ref[...]
        new_top = jnp.maximum(old_top, jnp.max(scores, axis=1, keepdims=True))
        weights = jnp.exp(scores - new_top)
        shrink = jnp.exp(old_top - new_top)
        top_ref[...] = new_top
        total_ref[...] = total_ref[...] * shrink + jnp.sum(weights, axis=1, keepdims=True)
        accum_ref[...] = accum_ref[...] * shrink + matmul(weights.astype(jnp.bfloat16), values)
        return carry

    lax.fori_loop(first_ref[qblock], qblock + 1, key_step, 0)
    total = total_ref[...]
    mixed = side_by_side((accum_ref[...] / total).astype(jnp.bfloat16), heads)
    mixed_ref[...] = mixed
    stats_ref[...] = jnp.broadcast_to(top_ref[...] + jnp.log(total), (heads * block, 128))
    part_ref[...] = matmul(mixed, outproj_ref[...]).astype(jnp.bfloat16)


def attention_forward(joined, starts, cosine, sine, query_up, out_proj, first_keys, block):
    group, width = joined.shape
    heads = query_up.shape[1] // DH
    model = out_proj.shape[1]
    count = group // block

    def whole(shape):
        return pl.BlockSpec(shape, lambda i, first: (0, 0), pipeline_mode=pl.Buffered(1))

    def rowed(cols, rows=block):
        return pl.BlockSpec((rows, cols), lambda i, first: (i, 0))

    pairs = group * group * heads // 4
    return pl.pallas_call(
        functools.partial(forward_kernel, heads, block),
        grid_spec=pltpu.PrefetchScalarGridSpec(
            num_scalar_prefetch=1,
            grid=(count,),
            in_specs=[
                whole((group, width)),
                rowed(1),
                rowed(HALF),
                rowed(HALF),
                whole(query_up.shape),
                whole(out_proj.shape),
            ],
            out_specs=[
                rowed(model),
                rowed(heads * DH),
                rowed(heads * DH),
                rowed(128, heads * block),
            ],
            scratch_shapes=[
                pltpu.VMEM((heads * block, 1), jnp.float32),
                pltpu.VMEM((heads * block, 1), jnp.float32),
                pltpu.VMEM((heads * block, DH), jnp.float32),
            ],
        ),
        out_shape=[
            jax.ShapeDtypeStruct((group, model), jnp.bfloat16),
            jax.ShapeDtypeStruct((group, heads * DH), jnp.bfloat16),
            jax.ShapeDtypeStruct((group, heads * DH), jnp.bfloat16),
            jax.ShapeDtypeStruct((group * heads, 128), jnp.float32),
        ],
        compiler_params=pltpu.CompilerParams(
            dimension_semantics=("arbitrary",), vmem_limit_bytes=48 * 1024 * 1024
        ),
        cost_estimate=pl.CostEstimate(
            flops=2 * group * heads * DH * (QR + model) + 4 * pairs * DH,
            transcendentals=pairs,
            bytes_accessed=2 * (joined.size + query_up.size + out_proj.size)
            + 2 * group * (model + 2 * heads * DH)
            + 4 * group * heads * 128
            + 8 * group * HALF,
        ),
        name="attention_forward",
    )(first_keys, joined, starts, cosine, sine, query_up, out_proj)


def backward_kernel(
    heads,
    block,
    first_ref,
    joined_ref,
    starts_ref,
    cos_ref,
    sin_ref,
    queryup_ref,
    outproj_ref,
    query_ref,
    mixed_ref,
    stats_ref,
    grad_ref,
    part_ref,
    gradq_ref,
    keyacc_ref,
    valueacc_ref,
    accum_ref,
):
    qblock = pl.program_id(0)
    query_row = pl.multiple_of(qblock * block, block)

    @pl.when(qblock == 0)
    def _():
        keyacc_ref[...] = jnp.zeros_like(keyacc_ref)
        valueacc_ref[...] = jnp.zeros_like(valueacc_ref)

    grad_mixed = contract(grad_ref[...], outproj_ref[...]).astype(jnp.bfloat16)
    products = grad_mixed.astype(jnp.float32) * mixed_ref[...].astype(jnp.float32)
    dots = jnp.sum(stacked(products, heads), axis=1, keepdims=True)
    grads = stacked(grad_mixed, heads)
    rows = stacked(query_ref[...], heads)
    level = stats_ref[:, 0:1]
    starts = starts_ref[...]
    accum_ref[...] = jnp.zeros_like(accum_ref)

    def key_step(kblock, carry):
        key_row = pl.multiple_of(kblock * block, block)
        keys = joined_ref[pl.ds(key_row, block), QR : QR + DH]
        values = joined_ref[pl.ds(key_row, block), QR + DH :]
        scores = contract(rows, keys)
        allowed = block_mask(starts, query_row, key_row, heads, block, block)
        weights = jnp.exp(jnp.where(allowed, scores, NEG) - level)
        grad_weights = contract(grads, values)
        grad_scores = (weights * (grad_weights - dots)).astype(jnp.bfloat16)
        accum_ref[...] += matmul(grad_scores, keys)
        keyacc_ref[pl.ds(key_row, block), :] += transposed(grad_scores, rows)
        valueacc_ref[pl.ds(key_row, block), :] += transposed(weights.astype(jnp.bfloat16), grads)
        return carry

    lax.fori_loop(first_ref[qblock], qblock + 1, key_step, 0)
    cosine = cos_ref[...]
    sine = sin_ref[...]
    grad_turned = side_by_side(accum_ref[...] * DH**-0.5, heads)
    back = []
    for h in range(heads):
        one = grad_turned[:, h * DH : h * DH + HALF]
        two = grad_turned[:, h * DH + HALF : (h + 1) * DH]
        back += [one * cosine + two * sine, two * cosine - one * sine]
    grad_query = jnp.concatenate(back, axis=1).astype(jnp.bfloat16)
    gradq_ref[...] = grad_query
    part_ref[pl.ds(query_row, block), :QR] = contract(grad_query, queryup_ref[...]).astype(
        jnp.bfloat16
    )

    @pl.when(qblock == pl.num_programs(0) - 1)
    def _():
        part_ref[:, QR : QR + DH] = keyacc_ref[...].astype(jnp.bfloat16)
        part_ref[:, QR + DH :] = valueacc_ref[...].astype(jnp.bfloat16)


def attention_backward(
    joined, starts, cosine, sine, query_up, out_proj, queries, mixed, stats, grads, first_keys, block
):
    group, width = joined.shape
    heads = query_up.shape[1] // DH
    model = out_proj.shape[1]
    count = group // block

    def whole(shape):
        return pl.BlockSpec(shape, lambda i, first: (0, 0), pipeline_mode=pl.Buffered(1))

    def rowed(cols, rows=block):
        return pl.BlockSpec((rows, cols), lambda i, first: (i, 0))

    pairs = group * group * heads // 4
    return pl.pallas_call(
        functools.partial(backward_kernel, heads, block),
        grid_spec=pltpu.PrefetchScalarGridSpec(
            num_scalar_prefetch=1,
            grid=(count,),
            in_specs=[
                whole((group, width)),
                rowed(1),
                rowed(HALF),
                rowed(HALF),
                whole(query_up.shape),
                whole(out_proj.shape),
                rowed(heads * DH),
                rowed(heads * DH),
                rowed(128, heads * block),
                rowed(model),
            ],
            out_specs=[
                pl.BlockSpec((group, width), lambda i, first: (0, 0)),
                rowed(heads * DH),
            ],
            scratch_shapes=[
                pltpu.VMEM((group, DH), jnp.float32),
                pltpu.VMEM((group, DH), jnp.float32),
                pltpu.VMEM((heads * block, DH), jnp.float32),
            ],
        ),
        out_shape=[
            jax.ShapeDtypeStruct((group, width), jnp.bfloat16),
            jax.ShapeDtypeStruct((group, heads * DH), jnp.bfloat16),
        ],
        compiler_params=pltpu.CompilerParams(
            dimension_semantics=("arbitrary",), vmem_limit_bytes=56 * 1024 * 1024
        ),
        cost_estimate=pl.CostEstimate(
            flops=2 * group * heads * DH * (QR + model) + 10 * pairs * DH,
            transcendentals=pairs,
            bytes_accessed=2 * (2 * joined.size + query_up.size + out_proj.size)
            + 2 * group * (model + 3 * heads * DH)
            + 4 * group * heads * 128
            + 8 * group * HALF,
        ),
        name="attention_backward",
    )(
        first_keys,
        joined,
        starts,
        cosine,
        sine,
        query_up,
        out_proj,
        queries,
        mixed,
        stats,
        grads,
    )


def tie(value, *others):
    return lax.optimization_barrier((value,) + others)[0]


def exchange(pieces, place, count):
    arrived = [lax.dynamic_index_in_dim(pieces, place, 0, keepdims=False)]
    for shift in range(1, count):
        sent = lax.dynamic_index_in_dim(
            pieces, lax.rem(place + shift, count), 0, keepdims=False
        )
        route = [(i, (i + shift) % count) for i in range(count)]
        arrived.append(lax.ppermute(sent, "head", route))
    stack = jnp.stack(arrived)
    order = lax.rem(place - jnp.arange(count, dtype=jnp.int32) + count, count)
    return jnp.stack(
        [lax.dynamic_index_in_dim(stack, order[i], 0, keepdims=False) for i in range(count)]
    )


def feed_kernel(
    normed_ref, cot_ref, gu_ref, down_ref, nmlp_ref, out_ref, act_ref, ggate_ref, gup_ref
):
    pieces, _, depth, _ = gu_ref.shape
    normed = normed_ref[...]
    gate = matmul(normed[:, :depth], gu_ref[0, 0])
    up = matmul(normed[:, :depth], gu_ref[0, 1])
    for s in range(1, pieces):
        part = normed[:, s * depth : (s + 1) * depth]
        gate += matmul(part, gu_ref[s, 0])
        up += matmul(part, gu_ref[s, 1])
    grad_act = contract(cot_ref[...], down_ref[...])
    sigmoid = 1.0 / (1.0 + jnp.exp(-gate))
    silu = gate * sigmoid
    activated = (silu * up).astype(jnp.bfloat16)
    act_ref[...] = activated
    grad_gate = (grad_act * up * (sigmoid * (1.0 + gate * (1.0 - sigmoid)))).astype(jnp.bfloat16)
    grad_up = (grad_act * silu).astype(jnp.bfloat16)
    ggate_ref[...] = grad_gate
    gup_ref[...] = grad_up
    for s in range(pieces):
        back = contract(grad_gate, gu_ref[s, 0]) + contract(grad_up, gu_ref[s, 1])
        nmlp_ref[:, s * depth : (s + 1) * depth] = back.astype(jnp.bfloat16)
    out_ref[...] = matmul(activated, down_ref[...]).astype(jnp.bfloat16)


def feed_forward(normed, cot, weight_gu, weight_down, block):
    group, model = normed.shape
    units = weight_down.shape[0]

    def rowed(cols):
        return pl.BlockSpec((block, cols), lambda i: (i, 0))

    return pl.pallas_call(
        feed_kernel,
        grid=(group // block,),
        in_specs=[
            rowed(model),
            rowed(model),
            pl.BlockSpec(weight_gu.shape, lambda i: (0, 0, 0, 0), pipeline_mode=pl.Buffered(1)),
            pl.BlockSpec(weight_down.shape, lambda i: (0, 0), pipeline_mode=pl.Buffered(1)),
        ],
        out_specs=[rowed(model), rowed(model), rowed(units), rowed(units), rowed(units)],
        out_shape=[
            jax.ShapeDtypeStruct((group, model), jnp.bfloat16),
            jax.ShapeDtypeStruct((group, model), jnp.bfloat16),
            jax.ShapeDtypeStruct((group, units), jnp.bfloat16),
            jax.ShapeDtypeStruct((group, units), jnp.bfloat16),
            jax.ShapeDtypeStruct((group, units), jnp.bfloat16),
        ],
        compiler_params=pltpu.CompilerParams(
            dimension_semantics=("arbitrary",), vmem_limit_bytes=56 * 1024 * 1024
        ),
        cost_estimate=pl.CostEstimate(
            flops=12 * group * model * units,
            transcendentals=group * units,
            bytes_accessed=2 * (4 * group * model + 3 * group * units + 3 * model * units),
        ),
        name="feed_forward",
    )(normed, cot, weight_gu, weight_down)


def weights_kernel(left_ref, right_ref, out_ref):
    product = transposed(left_ref[...], right_ref[...])
    out_ref[...] = product.astype(jnp.bfloat16).reshape(out_ref.shape)


def weight_product(left, right, rows, cols, out_shape, out_block, out_map, height=None):
    tokens = left.shape[0]
    height = height or left.shape[1]
    width = right.shape[1]
    return pl.pallas_call(
        weights_kernel,
        grid=(height // rows, width // cols),
        in_specs=[
            pl.BlockSpec((tokens, rows), lambda i, j: (0, i)),
            pl.BlockSpec((tokens, cols), lambda i, j: (0, j)),
        ],
        out_specs=pl.BlockSpec(out_block, out_map),
        out_shape=jax.ShapeDtypeStruct(out_shape, jnp.bfloat16),
        compiler_params=pltpu.CompilerParams(
            dimension_semantics=("arbitrary", "arbitrary"), vmem_limit_bytes=40 * 1024 * 1024
        ),
        cost_estimate=pl.CostEstimate(
            flops=2 * tokens * height * width,
            transcendentals=0,
            bytes_accessed=2 * (tokens * (height + width) + height * width),
        ),
        name="weight_product",
    )(left, right)


def packed_kernel(left_ref, right_ref, gains_ref, out_ref):
    cols = right_ref.shape[1]
    out_ref[:, :cols] = transposed(left_ref[...], right_ref[...]).astype(jnp.bfloat16)
    out_ref[:, cols:] = gains_ref[...]


def packed_product(left, right, gains, rows):
    tokens, model = left.shape
    cols = right.shape[1]
    width = cols + gains.shape[1]
    return pl.pallas_call(
        packed_kernel,
        grid=(model // rows,),
        in_specs=[
            pl.BlockSpec((tokens, rows), lambda i: (0, i)),
            pl.BlockSpec((tokens, cols), lambda i: (0, 0)),
            pl.BlockSpec((rows, gains.shape[1]), lambda i: (i, 0)),
        ],
        out_specs=pl.BlockSpec((rows, width), lambda i: (i, 0)),
        out_shape=jax.ShapeDtypeStruct((model, width), jnp.bfloat16),
        compiler_params=pltpu.CompilerParams(
            dimension_semantics=("arbitrary",), vmem_limit_bytes=32 * 1024 * 1024
        ),
        cost_estimate=pl.CostEstimate(
            flops=2 * tokens * model * cols,
            transcendentals=0,
            bytes_accessed=2 * (left.size + right.size + model * width),
        ),
        name="packed_product",
    )(left, right, gains)


def gu_kernel(left_ref, gate_ref, up_ref, out_ref):
    left = left_ref[...]
    out_ref[0, 0] = transposed(left, gate_ref[...]).astype(jnp.bfloat16)
    out_ref[0, 1] = transposed(left, up_ref[...]).astype(jnp.bfloat16)


def gu_product(normed, grad_gate, grad_up, pieces, split):
    tokens, model = normed.shape
    units = grad_gate.shape[1]
    depth = model // pieces
    rows = depth // split
    return pl.pallas_call(
        gu_kernel,
        grid=(pieces, split),
        in_specs=[
            pl.BlockSpec((tokens, rows), lambda s, i: (0, s * split + i)),
            pl.BlockSpec((tokens, units), lambda s, i: (0, 0), pipeline_mode=pl.Buffered(1)),
            pl.BlockSpec((tokens, units), lambda s, i: (0, 0), pipeline_mode=pl.Buffered(1)),
        ],
        out_specs=pl.BlockSpec((1, 2, rows, units), lambda s, i: (s, 0, i, 0)),
        out_shape=jax.ShapeDtypeStruct((pieces, 2, depth, units), jnp.bfloat16),
        compiler_params=pltpu.CompilerParams(
            dimension_semantics=("arbitrary", "arbitrary"), vmem_limit_bytes=40 * 1024 * 1024
        ),
        cost_estimate=pl.CostEstimate(
            flops=4 * tokens * model * units,
            transcendentals=0,
            bytes_accessed=2 * (normed.size + 2 * grad_gate.size + 2 * model * units),
        ),
        name="gu_product",
    )(normed, grad_gate, grad_up)


def shards(
    inputs,
    segments,
    cotangent,
    norm_attn,
    attn_in,
    norm_latent,
    query_up,
    out_proj,
    norm_mlp,
    gate_up,
    down_proj,
):
    head_count = lax.axis_size("head")
    head_place = lax.axis_index("head")
    shard_rows, model = inputs.shape
    group_rows = shard_rows * head_count
    block_rows = min(512, group_rows)
    seq_count = lax.axis_size("seq")
    own_rows = attn_in.shape[0]
    own_latent = norm_latent.shape[0]
    own_units = down_proj.shape[0]
    units = seq_count * own_units
    device_count = seq_count * head_count
    proj_cols = attn_in.shape[1]
    gain_cols = jnp.stack(
        [norm_attn, norm_mlp, jnp.pad(norm_latent, (0, own_rows - own_latent))], axis=1
    )
    packed = jnp.concatenate([attn_in, jnp.pad(gain_cols, ((0, 0), (0, 125)))], axis=1)
    packed_all = lax.all_gather(packed, ("seq", "head"), axis=0, tiled=True)
    pieces = gate_up.reshape(own_rows, 2, seq_count, head_count, own_units)
    pieces = pieces.transpose(3, 1, 0, 2, 4).reshape(head_count, 2, own_rows, units)
    turned = exchange(pieces, head_place, head_count)
    turned = turned.transpose(1, 0, 2, 3).reshape(1, 2, head_count * own_rows, units)
    weight_gu = lax.all_gather(turned, "seq", axis=0, tiled=True)
    weight_down = lax.all_gather(down_proj, "seq", axis=0, tiled=True)
    cot_all = lax.all_gather(cotangent, "head", axis=0, tiled=True)
    packed_all = tie(packed_all, cot_all, turned)
    weight_in = packed_all[:, :proj_cols]
    gain_attn = packed_all[:, proj_cols].astype(jnp.float32)
    gain_mlp = packed_all[:, proj_cols + 1].astype(jnp.float32)
    gain_latent = (
        packed_all[:, proj_cols + 2]
        .reshape(device_count, own_rows)[:, :own_latent]
        .reshape(device_count * own_latent)
        .astype(jnp.float32)
    )
    starts = segment_starts(segments[0])
    first_keys = starts[::block_rows] // block_rows
    cosine, sine = angles(starts)
    row_start = head_place * shard_rows
    cos_local = lax.dynamic_slice_in_dim(cosine, row_start, shard_rows, 0)
    sin_local = lax.dynamic_slice_in_dim(sine, row_start, shard_rows, 0)
    inputs_f = inputs.astype(jnp.float32)
    normed = rms_norm(inputs_f, gain_attn).astype(jnp.bfloat16)
    projected = jnp.dot(normed, weight_in, preferred_element_type=jnp.float32)
    latent = projected[:, :QR]
    key_raw = projected[:, QR : QR + DH]
    latent_n = rms_norm(latent, gain_latent).astype(jnp.bfloat16)
    keys_local = rotary(key_raw, cos_local, sin_local).astype(jnp.bfloat16)
    values_local = projected[:, QR + DH :].astype(jnp.bfloat16)
    joined_all = lax.all_gather(
        jnp.concatenate([latent_n, keys_local, values_local], axis=1), "head", axis=0, tiled=True
    )
    joined_all = tie(joined_all, weight_gu, weight_down)
    attn_part, queries, mixed, stats = attention_forward(
        joined_all, starts[:, None], cosine, sine, query_up, out_proj, first_keys, block_rows
    )
    attn_out = lax.psum_scatter(
        attn_part,
        "head",
        scatter_dimension=0,
        tiled=True,
    ).astype(jnp.float32)
    hidden = inputs_f + attn_out
    normed_mlp = rms_norm(hidden, gain_mlp).astype(jnp.bfloat16)
    nmlp_all = lax.all_gather(normed_mlp, "head", axis=0, tiled=True)
    nmlp_part, down_part, activated, grad_gate, grad_up = feed_forward(
        nmlp_all, cot_all, weight_gu, weight_down, 256
    )
    grad_nmlp = lax.psum_scatter(nmlp_part, "head", scatter_dimension=0, tiled=True)
    gu_part = gu_product(nmlp_all, grad_gate, grad_up, seq_count, 2)
    down_grad = weight_product(
        activated,
        cot_all,
        units,
        512,
        (seq_count, own_units, model),
        (seq_count, own_units, 512),
        lambda i, j: (0, 0, j),
    )
    grad_nmlp = tie(grad_nmlp, gu_part, down_grad).astype(jnp.float32)
    down_out = lax.psum_scatter(down_part, "head", scatter_dimension=0, tiled=True)
    gu_rows = lax.psum_scatter(gu_part, "seq", scatter_dimension=0, tiled=True)
    down_rows = lax.psum_scatter(down_grad, "seq", scatter_dimension=0, tiled=True)
    norm_value, mlp_back = jax.vjp(rms_norm, hidden, gain_mlp)
    grad_hidden_n, mlpnorm_part = mlp_back(grad_nmlp)
    grad_hidden = cotangent.astype(jnp.float32) + grad_hidden_n
    grad_attn = grad_hidden.astype(jnp.bfloat16)
    grad_attn_all = lax.all_gather(grad_attn, "head", axis=0, tiled=True)
    grad_part, grad_query = attention_backward(
        joined_all,
        starts[:, None],
        cosine,
        sine,
        query_up,
        out_proj,
        queries,
        mixed,
        stats,
        grad_attn_all,
        first_keys,
        block_rows,
    )
    received = lax.psum_scatter(grad_part, "head", scatter_dimension=0, tiled=True)
    head_cols = query_up.shape[1]
    queryup_part = weight_product(
        joined_all,
        grad_query,
        QR // seq_count,
        head_cols,
        (seq_count, QR // seq_count, head_cols),
        (1, QR // seq_count, head_cols),
        lambda i, j: (i, 0, 0),
        height=QR,
    )
    outproj_part = weight_product(
        mixed,
        grad_attn_all,
        head_cols,
        model // seq_count,
        (seq_count, head_cols, model // seq_count),
        (1, head_cols, model // seq_count),
        lambda i, j: (j, 0, 0),
    )
    received = tie(received, queryup_part, outproj_part, down_out, gu_rows, down_rows)
    received = received.astype(jnp.float32)
    grad_latent_n, grad_keys, grad_values = (
        received[:, :QR],
        received[:, QR : QR + DH],
        received[:, QR + DH :],
    )
    layer_out = (hidden + down_out.astype(jnp.float32)).astype(jnp.bfloat16)
    downproj_grad = down_rows[0].astype(jnp.float32)
    queryup_grad = lax.psum_scatter(queryup_part, "seq", scatter_dimension=0, tiled=True)
    queryup_grad = queryup_grad[0].astype(jnp.float32)
    outproj_grad = lax.psum_scatter(outproj_part, "seq", scatter_dimension=0, tiled=True)
    outproj_grad = outproj_grad[0].astype(jnp.float32)
    gu_back = exchange(
        gu_rows.reshape(2, head_count, own_rows, units).transpose(1, 0, 2, 3),
        head_place,
        head_count,
    )
    gateup_grad = (
        gu_back.reshape(head_count, 2, own_rows, seq_count, own_units)
        .transpose(2, 1, 3, 0, 4)
        .reshape(own_rows, 2 * device_count * own_units)
        .astype(jnp.float32)
    )
    latent_value, latent_back = jax.vjp(rms_norm, latent, gain_latent)
    grad_latent, latnorm_part = latent_back(grad_latent_n)
    turned_key, key_back = jax.vjp(lambda key_in: rotary(key_in, cos_local, sin_local), key_raw)
    (grad_key_raw,) = key_back(grad_keys)
    grad_proj = jnp.concatenate([grad_latent, grad_key_raw, grad_values], axis=1).astype(
        jnp.bfloat16
    )
    grad_normed = contract(grad_proj, weight_in)
    input_value, input_back = jax.vjp(rms_norm, inputs_f, gain_attn)
    grad_input_n, attnnorm_part = input_back(grad_normed)
    input_grad = grad_hidden + grad_input_n
    latent_col = jnp.pad(
        latnorm_part.reshape(device_count, own_latent), ((0, 0), (0, own_rows - own_latent))
    ).reshape(device_count * own_rows)
    gain_parts = jnp.stack([attnnorm_part, mlpnorm_part, latent_col], axis=1)
    gain_parts = jnp.pad(gain_parts, ((0, 0), (0, 125))).astype(jnp.bfloat16)
    packed_part = packed_product(normed, grad_proj, gain_parts, min(512, model))
    packed_rows = lax.psum_scatter(packed_part, "seq", scatter_dimension=0, tiled=True)
    packed_grad = lax.psum_scatter(
        packed_rows, "head", scatter_dimension=0, tiled=True
    ).astype(jnp.float32)
    attnin_grad = packed_grad[:, :proj_cols]
    attnnorm_grad = packed_grad[:, proj_cols]
    mlpnorm_grad = packed_grad[:, proj_cols + 1]
    latnorm_grad = packed_grad[:own_latent, proj_cols + 2]
    return (
        layer_out,
        input_grad,
        attnnorm_grad,
        attnin_grad,
        latnorm_grad,
        queryup_grad,
        outproj_grad,
        mlpnorm_grad,
        gateup_grad,
        downproj_grad,
    )


def solution(mesh):
    in_specs = (
        P(("seq", "head"), None),
        P("seq", None),
        P(("seq", "head"), None),
        P(("seq", "head")),
        P(("seq", "head"), None),
        P(("seq", "head")),
        P(None, "head"),
        P("head", None),
        P(("seq", "head")),
        P(("seq", "head"), None),
        P(("seq", "head"), None),
    )
    out_specs = (
        P(("seq", "head"), None),
        P(("seq", "head"), None),
        P(("seq", "head")),
        P(("seq", "head"), None),
        P(("seq", "head")),
        P("seq", "head"),
        P("head", "seq"),
        P(("seq", "head")),
        P(("seq", "head"), None),
        P(("seq", "head"), None),
    )
    return jax.shard_map(shards, mesh=mesh, in_specs=in_specs, out_specs=out_specs, check_vma=False)
```

```python
import functools

import jax
import jax.numpy as jnp
from jax import lax
from jax.experimental import pallas as pl
from jax.experimental.pallas import tpu as pltpu
from jax.sharding import PartitionSpec as P

DH = 256
QR = 1024
HALF = DH // 2


EPS = 1e-06
THETA = 10000.0
NEG = -1e30


def contract(left, right):
    return lax.dot_general(
        left, right, (((1,), (1,)), ((), ())), preferred_element_type=jnp.float32
    )


def transposed(left, right):
    return lax.dot_general(
        left, right, (((0,), (0,)), ((), ())), preferred_element_type=jnp.float32
    )


def matmul(left, right):
    return jnp.dot(left, right, preferred_element_type=jnp.float32)


def rms_norm(values_in, gain_vec):
    return (
        values_in
        * lax.rsqrt(jnp.mean(values_in * values_in, axis=-1, keepdims=True) + EPS)
        * gain_vec
    )


def rotary(values_in, cosine, sine):
    half_dim = values_in.shape[-1] // 2
    first_half = values_in[..., :half_dim]
    second_half = values_in[..., half_dim:]
    return jnp.concatenate(
        [first_half * cosine - second_half * sine, second_half * cosine + first_half * sine],
        axis=-1,
    )


def segment_starts(segment_row):
    index = jnp.arange(segment_row.shape[0], dtype=jnp.int32)
    opens = jnp.concatenate([jnp.ones((1,), jnp.bool_), segment_row[1:] != segment_row[:-1]])
    return lax.cummax(jnp.where(opens, index, jnp.zeros_like(index)), axis=0)


def angles(starts):
    index = jnp.arange(starts.shape[0], dtype=jnp.int32)
    places = (index - starts).astype(jnp.float32)
    exponent = jnp.arange(DH // 2, dtype=jnp.float32) * (-2.0 / DH)
    frequency = jnp.power(jnp.float32(THETA), exponent)
    turned = places[:, None] * frequency[None, :]
    return (jnp.cos(turned), jnp.sin(turned))


def stacked(values_in, heads):
    return jnp.concatenate([values_in[:, h * DH : (h + 1) * DH] for h in range(heads)], axis=0)


def side_by_side(values_in, heads):
    rows = values_in.shape[0] // heads
    return jnp.concatenate([values_in[h * rows : (h + 1) * rows] for h in range(heads)], axis=1)


def block_mask(starts, query_row, key_row, heads, rows, cols):
    place_query = query_row + lax.broadcasted_iota(jnp.int32, (rows, cols), 0)
    place_key = key_row + lax.broadcasted_iota(jnp.int32, (rows, cols), 1)
    allowed = (place_key >= starts) & (place_key <= place_query)
    return jnp.concatenate([allowed] * heads, axis=0) if heads > 1 else allowed


def forward_kernel(
    heads,
    block,
    first_ref,
    joined_ref,
    starts_ref,
    cos_ref,
    sin_ref,
    queryup_ref,
    outproj_ref,
    part_ref,
    query_ref,
    mixed_ref,
    stats_ref,
    top_ref,
    total_ref,
    accum_ref,
):
    qblock = pl.program_id(0)
    query_row = pl.multiple_of(qblock * block, block)
    cosine = cos_ref[...]
    sine = sin_ref[...]
    raw = matmul(joined_ref[pl.ds(query_row, block), :QR], queryup_ref[...])
    turned = []
    for h in range(heads):
        one = raw[:, h * DH : h * DH + HALF]
        two = raw[:, h * DH + HALF : (h + 1) * DH]
        turned += [one * cosine - two * sine, two * cosine + one * sine]
    queries = (jnp.concatenate(turned, axis=1)).astype(jnp.bfloat16) * jnp.bfloat16(DH**-0.5)
    query_ref[...] = queries
    rows = stacked(queries, heads)
    starts = starts_ref[...]
    top_ref[...] = jnp.full_like(top_ref, NEG)
    total_ref[...] = jnp.zeros_like(total_ref)
    accum_ref[...] = jnp.zeros_like(accum_ref)

    def key_step(kblock, carry):
        key_row = pl.multiple_of(kblock * block, block)
        keys = joined_ref[pl.ds(key_row, block), QR : QR + DH]
        values = joined_ref[pl.ds(key_row, block), QR + DH :]
        scores = contract(rows, keys)
        allowed = block_mask(starts, query_row, key_row, heads, block, block)
        scores = jnp.where(allowed, scores, NEG)
        old_top = top_ref[...]
        new_top = jnp.maximum(old_top, jnp.max(scores, axis=1, keepdims=True))
        weights = jnp.exp(scores - new_top)
        shrink = jnp.exp(old_top - new_top)
        top_ref[...] = new_top
        total_ref[...] = total_ref[...] * shrink + jnp.sum(weights, axis=1, keepdims=True)
        accum_ref[...] = accum_ref[...] * shrink + matmul(weights.astype(jnp.bfloat16), values)
        return carry

    lax.fori_loop(first_ref[qblock], qblock + 1, key_step, 0)
    total = total_ref[...]
    mixed = side_by_side((accum_ref[...] / total).astype(jnp.bfloat16), heads)
    mixed_ref[...] = mixed
    stats_ref[...] = jnp.broadcast_to(top_ref[...] + jnp.log(total), (heads * block, 128))
    part_ref[...] = matmul(mixed, outproj_ref[...]).astype(jnp.bfloat16)


def attention_forward(joined, starts, cosine, sine, query_up, out_proj, first_keys, block):
    group, width = joined.shape
    heads = query_up.shape[1] // DH
    model = out_proj.shape[1]
    count = group // block

    def whole(shape):
        return pl.BlockSpec(shape, lambda i, first: (0, 0), pipeline_mode=pl.Buffered(1))

    def rowed(cols, rows=block):
        return pl.BlockSpec((rows, cols), lambda i, first: (i, 0))

    pairs = group * group * heads // 4
    return pl.pallas_call(
        functools.partial(forward_kernel, heads, block),
        grid_spec=pltpu.PrefetchScalarGridSpec(
            num_scalar_prefetch=1,
            grid=(count,),
            in_specs=[
                whole((group, width)),
                rowed(1),
                rowed(HALF),
                rowed(HALF),
                whole(query_up.shape),
                whole(out_proj.shape),
            ],
            out_specs=[
                rowed(model),
                rowed(heads * DH),
                rowed(heads * DH),
                rowed(128, heads * block),
            ],
            scratch_shapes=[
                pltpu.VMEM((heads * block, 1), jnp.float32),
                pltpu.VMEM((heads * block, 1), jnp.float32),
                pltpu.VMEM((heads * block, DH), jnp.float32),
            ],
        ),
        out_shape=[
            jax.ShapeDtypeStruct((group, model), jnp.bfloat16),
            jax.ShapeDtypeStruct((group, heads * DH), jnp.bfloat16),
            jax.ShapeDtypeStruct((group, heads * DH), jnp.bfloat16),
            jax.ShapeDtypeStruct((group * heads, 128), jnp.float32),
        ],
        compiler_params=pltpu.CompilerParams(
            dimension_semantics=("arbitrary",), vmem_limit_bytes=48 * 1024 * 1024
        ),
        cost_estimate=pl.CostEstimate(
            flops=2 * group * heads * DH * (QR + model) + 4 * pairs * DH,
            transcendentals=pairs,
            bytes_accessed=2 * (joined.size + query_up.size + out_proj.size)
            + 2 * group * (model + 2 * heads * DH)
            + 4 * group * heads * 128
            + 8 * group * HALF,
        ),
        name="attention_forward",
    )(first_keys, joined, starts, cosine, sine, query_up, out_proj)


def backward_kernel(
    heads,
    block,
    first_ref,
    joined_ref,
    starts_ref,
    cos_ref,
    sin_ref,
    queryup_ref,
    outproj_ref,
    query_ref,
    mixed_ref,
    stats_ref,
    grad_ref,
    part_ref,
    gradq_ref,
    keyacc_ref,
    valueacc_ref,
    accum_ref,
):
    qblock = pl.program_id(0)
    query_row = pl.multiple_of(qblock * block, block)

    @pl.when(qblock == 0)
    def _():
        keyacc_ref[...] = jnp.zeros_like(keyacc_ref)
        valueacc_ref[...] = jnp.zeros_like(valueacc_ref)

    grad_mixed = contract(grad_ref[...], outproj_ref[...]).astype(jnp.bfloat16)
    products = grad_mixed.astype(jnp.float32) * mixed_ref[...].astype(jnp.float32)
    dots = jnp.sum(stacked(products, heads), axis=1, keepdims=True)
    grads = stacked(grad_mixed, heads)
    rows = stacked(query_ref[...], heads)
    level = stats_ref[:, 0:1]
    starts = starts_ref[...]
    accum_ref[...] = jnp.zeros_like(accum_ref)

    def key_step(kblock, carry):
        key_row = pl.multiple_of(kblock * block, block)
        keys = joined_ref[pl.ds(key_row, block), QR : QR + DH]
        values = joined_ref[pl.ds(key_row, block), QR + DH :]
        scores = contract(rows, keys)
        allowed = block_mask(starts, query_row, key_row, heads, block, block)
        weights = jnp.exp(jnp.where(allowed, scores, NEG) - level)
        grad_weights = contract(grads, values)
        grad_scores = (weights * (grad_weights - dots)).astype(jnp.bfloat16)
        accum_ref[...] += matmul(grad_scores, keys)
        keyacc_ref[pl.ds(key_row, block), :] += transposed(grad_scores, rows)
        valueacc_ref[pl.ds(key_row, block), :] += transposed(weights.astype(jnp.bfloat16), grads)
        return carry

    lax.fori_loop(first_ref[qblock], qblock + 1, key_step, 0)
    cosine = cos_ref[...]
    sine = sin_ref[...]
    grad_turned = side_by_side(accum_ref[...] * DH**-0.5, heads)
    back = []
    for h in range(heads):
        one = grad_turned[:, h * DH : h * DH + HALF]
        two = grad_turned[:, h * DH + HALF : (h + 1) * DH]
        back += [one * cosine + two * sine, two * cosine - one * sine]
    grad_query = jnp.concatenate(back, axis=1).astype(jnp.bfloat16)
    gradq_ref[...] = grad_query
    part_ref[pl.ds(query_row, block), :QR] = contract(grad_query, queryup_ref[...]).astype(
        jnp.bfloat16
    )

    @pl.when(qblock == pl.num_programs(0) - 1)
    def _():
        part_ref[:, QR : QR + DH] = keyacc_ref[...].astype(jnp.bfloat16)
        part_ref[:, QR + DH :] = valueacc_ref[...].astype(jnp.bfloat16)


def attention_backward(
    joined, starts, cosine, sine, query_up, out_proj, queries, mixed, stats, grads, first_keys, block
):
    group, width = joined.shape
    heads = query_up.shape[1] // DH
    model = out_proj.shape[1]
    count = group // block

    def whole(shape):
        return pl.BlockSpec(shape, lambda i, first: (0, 0), pipeline_mode=pl.Buffered(1))

    def rowed(cols, rows=block):
        return pl.BlockSpec((rows, cols), lambda i, first: (i, 0))

    pairs = group * group * heads // 4
    return pl.pallas_call(
        functools.partial(backward_kernel, heads, block),
        grid_spec=pltpu.PrefetchScalarGridSpec(
            num_scalar_prefetch=1,
            grid=(count,),
            in_specs=[
                whole((group, width)),
                rowed(1),
                rowed(HALF),
                rowed(HALF),
                whole(query_up.shape),
                whole(out_proj.shape),
                rowed(heads * DH),
                rowed(heads * DH),
                rowed(128, heads * block),
                rowed(model),
            ],
            out_specs=[
                pl.BlockSpec((group, width), lambda i, first: (0, 0)),
                rowed(heads * DH),
            ],
            scratch_shapes=[
                pltpu.VMEM((group, DH), jnp.float32),
                pltpu.VMEM((group, DH), jnp.float32),
                pltpu.VMEM((heads * block, DH), jnp.float32),
            ],
        ),
        out_shape=[
            jax.ShapeDtypeStruct((group, width), jnp.bfloat16),
            jax.ShapeDtypeStruct((group, heads * DH), jnp.bfloat16),
        ],
        compiler_params=pltpu.CompilerParams(
            dimension_semantics=("arbitrary",), vmem_limit_bytes=56 * 1024 * 1024
        ),
        cost_estimate=pl.CostEstimate(
            flops=2 * group * heads * DH * (QR + model) + 10 * pairs * DH,
            transcendentals=pairs,
            bytes_accessed=2 * (2 * joined.size + query_up.size + out_proj.size)
            + 2 * group * (model + 3 * heads * DH)
            + 4 * group * heads * 128
            + 8 * group * HALF,
        ),
        name="attention_backward",
    )(
        first_keys,
        joined,
        starts,
        cosine,
        sine,
        query_up,
        out_proj,
        queries,
        mixed,
        stats,
        grads,
    )


def tie(value, *others):
    return lax.optimization_barrier((value,) + others)[0]


MESH = pl.DeviceIdType.MESH
ANY = pl.BlockSpec(memory_space=pl.ANY)


def send(source, target, send_sem, recv_sem, place):
    return pltpu.make_async_remote_copy(
        src_ref=source,
        dst_ref=target,
        send_sem=send_sem,
        recv_sem=recv_sem,
        device_id={"head": place},
        device_id_type=MESH,
    )


def greet(place, spot, chips, sibling):
    barrier = pltpu.get_barrier_semaphore()
    pl.semaphore_signal(barrier, inc=1, device_id={"head": sibling}, device_id_type=MESH)

    @pl.when(spot > 0)
    def _():
        pl.semaphore_signal(barrier, inc=1, device_id={"head": place - 2}, device_id_type=MESH)

    @pl.when(spot < chips - 1)
    def _():
        pl.semaphore_signal(barrier, inc=1, device_id={"head": place + 2}, device_id_type=MESH)

    below = (spot + chips - 1) // chips
    above = (2 * chips - 2 - spot) // chips
    pl.semaphore_wait(barrier, 1 + below + above)


def line_places():
    place = lax.axis_index("head")
    chips = lax.axis_size("head") // 2
    spot = place // 2
    core = lax.rem(place, 2)
    return place, chips, spot, core, place + 1 - 2 * core


CUTS = 4


def gather_line(piece_ref, whole_ref, local_sem, up_sem, down_sem, side_sem, recv_sem):
    place, chips, spot, core, sibling = line_places()
    rows = piece_ref.shape[0] // CUTS

    def slot(chip, which, cut):
        return whole_ref.at[2 * chip + which, pl.ds(cut * rows, rows)]

    def mine(cut):
        return piece_ref.at[pl.ds(cut * rows, rows)]

    def up(chip, cut, source):
        received = recv_sem.at[2 * chip + core, cut]
        return send(source, slot(chip, core, cut), up_sem.at[chip, cut], received, place + 2)

    def down(chip, cut, source):
        received = recv_sem.at[2 * chip + core, cut]
        return send(source, slot(chip, core, cut), down_sem.at[chip, cut], received, place - 2)

    def side(chip, cut, source):
        received = recv_sem.at[2 * chip + core, cut]
        return send(source, slot(chip, core, cut), side_sem.at[chip, cut], received, sibling)

    own = pltpu.make_async_copy(piece_ref, whole_ref.at[place], local_sem)
    for cut in range(CUTS):

        @pl.when(spot < chips - 1)
        def _():
            up(spot, cut, mine(cut)).start()

        @pl.when(spot > 0)
        def _():
            down(spot, cut, mine(cut)).start()

    for cut in range(CUTS):
        side(spot, cut, mine(cut)).start()
    own.start()
    yield

    for k in range(1, chips):
        below = spot - k
        above = spot + k
        for cut in range(CUTS):

            @pl.when(below >= 0)
            def _():
                landed = slot(below, core, cut)
                up(below, cut, landed).wait_recv()

                @pl.when(spot < chips - 1)
                def _():
                    up(below, cut, landed).start()

                side(below, cut, landed).start()

            @pl.when(above < chips)
            def _():
                landed = slot(above, core, cut)
                down(above, cut, landed).wait_recv()

                @pl.when(spot > 0)
                def _():
                    down(above, cut, landed).start()

                side(above, cut, landed).start()

            yield

    own.wait()
    for chip in range(chips):
        for cut in range(CUTS):
            received = recv_sem.at[2 * chip + 1 - core, cut]
            send(
                mine(cut), slot(chip, 1 - core, cut), side_sem.at[chip, cut], received, sibling
            ).wait_recv()
            side(chip, cut, mine(cut)).wait_send()

            @pl.when((chip <= spot) & (spot < chips - 1))
            def _():
                up(chip, cut, mine(cut)).wait_send()

            @pl.when((chip >= spot) & (spot > 0))
            def _():
                down(chip, cut, mine(cut)).wait_send()


def together(*lines):
    active = list(lines)
    while active:
        active = [line for line in active if next(line, active) is None]


def gather_sems(chips):
    return [
        pltpu.SemaphoreType.DMA,
        pltpu.SemaphoreType.DMA((chips, CUTS)),
        pltpu.SemaphoreType.DMA((chips, CUTS)),
        pltpu.SemaphoreType.DMA((chips, CUTS)),
        pltpu.SemaphoreType.DMA((2 * chips, CUTS)),
    ]


def gather_kernel(piece_ref, whole_ref, *sems):
    place, chips, spot, core, sibling = line_places()
    greet(place, spot, chips, sibling)
    together(gather_line(piece_ref, whole_ref, *sems))


def gather_head(piece, head_count, collective_id):
    rows, width = piece.shape
    chips = head_count // 2
    whole = pl.pallas_call(
        gather_kernel,
        in_specs=[ANY],
        out_specs=ANY,
        out_shape=jax.ShapeDtypeStruct((head_count, rows, width), piece.dtype),
        scratch_shapes=gather_sems(chips),
        compiler_params=pltpu.CompilerParams(
            collective_id=collective_id, has_side_effects=True
        ),
        cost_estimate=pl.CostEstimate(
            flops=0, transcendentals=0, bytes_accessed=2 * head_count * rows * width * 20
        ),
        name="gather_head",
    )(piece)
    return whole.reshape(head_count * rows, width)


def reduce_line(
    part_ref,
    out_ref,
    own_buf,
    side_buf,
    below_buf,
    above_buf,
    load_sem,
    side_send,
    side_recv,
    up_send,
    up_recv,
    down_send,
    down_recv,
):
    place, chips, spot, core, sibling = line_places()
    rows = own_buf.shape[1] // CUTS

    def cut_of(ref, chip, cut):
        return ref.at[chip, pl.ds(cut * rows, rows)]

    def side(chip, cut):
        return send(
            cut_of(part_ref, 2 * chip + 1 - core, cut),
            cut_of(side_buf, chip, cut),
            side_send.at[chip, cut],
            side_recv.at[chip, cut],
            sibling,
        )

    def load(chip, cut):
        return pltpu.make_async_copy(
            cut_of(part_ref, 2 * chip + core, cut),
            cut_of(own_buf, chip, cut),
            load_sem.at[chip, cut],
        )

    def up(chip, cut):
        return send(
            cut_of(own_buf, chip, cut),
            cut_of(below_buf, chip, cut),
            up_send.at[chip, cut],
            up_recv.at[chip, cut],
            place + 2,
        )

    def down(chip, cut):
        return send(
            cut_of(own_buf, chip, cut),
            cut_of(above_buf, chip, cut),
            down_send.at[chip, cut],
            down_recv.at[chip, cut],
            place - 2,
        )

    order = []
    for k in range((chips + 1) // 2):
        order += [k] if k == chips - 1 - k else [chips - 1 - k, k]
    for chip in order:
        for cut in range(CUTS):
            side(chip, cut).start()
            load(chip, cut).start()
    yield

    def add(chip, cut, others, target):
        @pl.loop(0, rows // 16)
        def _(i):
            part = pl.ds(pl.multiple_of(cut * rows + i * 16, 16), 16)
            total = own_buf[chip, part, :].astype(jnp.float32)
            for other in others:
                total += other[chip, part, :].astype(jnp.float32)
            if target is None:
                own_buf[chip, part, :] = total.astype(own_buf.dtype)
            else:
                target[part, :] = total.astype(target.dtype)

    def ready(chip, cut):
        side(chip, cut).wait_recv()
        load(chip, cut).wait()

    for k in range(chips - 1):
        high = chips - 1 - k
        low = k
        for cut in range(CUTS):

            @pl.when(spot < high)
            def _():
                ready(high, cut)

                @pl.when(spot > 0)
                def _():
                    up(high, cut).wait_recv()
                    add(high, cut, [side_buf, below_buf], None)

                @pl.when(spot == 0)
                def _():
                    add(high, cut, [side_buf], None)

                up(high, cut).start()

            @pl.when(spot > low)
            def _():
                ready(low, cut)

                @pl.when(spot < chips - 1)
                def _():
                    down(low, cut).wait_recv()
                    add(low, cut, [side_buf, above_buf], None)

                @pl.when(spot == chips - 1)
                def _():
                    add(low, cut, [side_buf], None)

                down(low, cut).start()

            yield

    for chip in range(chips):

        @pl.when(spot == chip)
        def _():
            for cut in range(CUTS):
                ready(chip, cut)
                others = [side_buf]
                if chip > 0:
                    up(chip, cut).wait_recv()
                    others.append(below_buf)
                if chip < chips - 1:
                    down(chip, cut).wait_recv()
                    others.append(above_buf)
                add(chip, cut, others, out_ref)

        for cut in range(CUTS):
            side(chip, cut).wait_send()

            @pl.when(spot < chip)
            def _():
                up(chip, cut).wait_send()

            @pl.when(spot > chip)
            def _():
                down(chip, cut).wait_send()


def reduce_scratch(chips, rows, width):
    return [pltpu.VMEM((chips, rows, width), jnp.bfloat16)] * 4 + [
        pltpu.SemaphoreType.DMA((chips, CUTS))
    ] * 7


def reduce_kernel(part_ref, out_ref, *scratch):
    place, chips, spot, core, sibling = line_places()
    greet(place, spot, chips, sibling)
    together(reduce_line(part_ref, out_ref, *scratch))


def reduce_head(part, head_count, collective_id):
    group, width = part.shape
    rows = group // head_count
    chips = head_count // 2
    return pl.pallas_call(
        reduce_kernel,
        in_specs=[ANY],
        out_specs=pl.BlockSpec(memory_space=pltpu.VMEM),
        out_shape=jax.ShapeDtypeStruct((rows, width), jnp.float32),
        scratch_shapes=reduce_scratch(chips, rows, width),
        compiler_params=pltpu.CompilerParams(
            collective_id=collective_id, has_side_effects=True, vmem_limit_bytes=48 * 1024 * 1024
        ),
        cost_estimate=pl.CostEstimate(
            flops=0, transcendentals=0, bytes_accessed=2 * head_count * rows * width * 20
        ),
        name="reduce_head",
    )(part.reshape(head_count, rows, width))


def greet_all(with_lines):
    barrier = pltpu.get_barrier_semaphore()
    waits = 0
    for axis in ("head", "seq") if with_lines else ("head",):
        own = lax.axis_index(axis)
        count = lax.axis_size(axis)
        for shift in range(1, count):
            peer = lax.rem(own + shift, count)
            pl.semaphore_signal(barrier, inc=1, device_id={axis: peer}, device_id_type=MESH)
        waits += count - 1
    pl.semaphore_wait(barrier, waits)


def swap_line(scatter, piece_ref, out_ref, local_sem, send_sem, recv_sem):
    place = lax.axis_index("head")
    count = lax.axis_size("head")
    rows = piece_ref.shape[2] if scatter else piece_ref.shape[1] // count

    def source(index):
        if scatter:
            return piece_ref.at[index]
        return piece_ref.at[:, pl.ds(pl.multiple_of(index * rows, rows), rows), :]

    def target(index):
        if scatter:
            return out_ref.at[:, pl.ds(pl.multiple_of(index * rows, rows), rows), :]
        return out_ref.at[index]

    own = pltpu.make_async_copy(source(place), target(place), local_sem)
    own.start()
    copies = []
    for shift in range(1, count):
        peer = lax.rem(place + shift, count)
        copy = send(
            source(peer), target(place), send_sem.at[shift], recv_sem.at[shift], peer
        )
        copy.start()
        copies.append(copy)
    yield
    own.wait()
    for copy in copies:
        copy.wait()


def swap_sems(count):
    return [
        pltpu.SemaphoreType.DMA,
        pltpu.SemaphoreType.DMA((count,)),
        pltpu.SemaphoreType.DMA((count,)),
    ]


def gather_mesh(piece_ref, whole_ref, local_sem, up_sem, down_sem, seq_sem, side_sem, recv_sem):
    place, chips, spot, core, sibling = line_places()
    line = lax.axis_index("seq")
    lines = lax.axis_size("seq")

    def slot(row, chip, which):
        return whole_ref.at[row, 2 * chip + which]

    def to(axis, where, row, chip, source, sem):
        return pltpu.make_async_remote_copy(
            src_ref=source,
            dst_ref=slot(row, chip, core),
            send_sem=sem,
            recv_sem=recv_sem.at[row, 2 * chip + core],
            device_id={axis: where},
            device_id_type=MESH,
        )

    def up(chip, source):
        return to("head", place + 2, line, chip, source, up_sem.at[chip])

    def down(chip, source):
        return to("head", place - 2, line, chip, source, down_sem.at[chip])

    def across(shift, chip, source):
        where = lax.rem(line + shift, lines)
        return to("seq", where, line, chip, source, seq_sem.at[shift, chip])

    def side(row, chip, source):
        return to("head", sibling, row, chip, source, side_sem.at[row, chip])

    def spread(chip, source):
        for shift in range(1, lines):
            across(shift, chip, source).start()
        side(line, chip, source).start()

    own = pltpu.make_async_copy(piece_ref, slot(line, spot, core), local_sem)

    @pl.when(spot < chips - 1)
    def _():
        up(spot, piece_ref).start()

    @pl.when(spot > 0)
    def _():
        down(spot, piece_ref).start()

    spread(spot, piece_ref)
    own.start()
    yield

    for k in range(1, chips):
        below = spot - k
        above = spot + k

        @pl.when(below >= 0)
        def _():
            landed = slot(line, below, core)
            up(below, landed).wait_recv()

            @pl.when(spot < chips - 1)
            def _():
                up(below, landed).start()

            spread(below, landed)

        @pl.when(above < chips)
        def _():
            landed = slot(line, above, core)
            down(above, landed).wait_recv()

            @pl.when(spot > 0)
            def _():
                down(above, landed).start()

            spread(above, landed)

        yield

    for chip in range(chips):
        for shift in range(1, lines):
            row = lax.rem(line + shift, lines)
            landed = slot(row, chip, core)
            to("seq", row, row, chip, landed, seq_sem.at[shift, chip]).wait_recv()
            side(row, chip, landed).start()
        yield

    own.wait()
    for chip in range(chips):
        for row in range(lines):
            landed = slot(row, chip, 1 - core)
            pltpu.make_async_remote_copy(
                src_ref=landed,
                dst_ref=landed,
                send_sem=side_sem.at[row, chip],
                recv_sem=recv_sem.at[row, 2 * chip + 1 - core],
                device_id={"head": sibling},
                device_id_type=MESH,
            ).wait_recv()
            side(row, chip, piece_ref).wait_send()
        for shift in range(1, lines):
            across(shift, chip, piece_ref).wait_send()

        @pl.when((chip <= spot) & (spot < chips - 1))
        def _():
            up(chip, piece_ref).wait_send()

        @pl.when((chip >= spot) & (spot > 0))
        def _():
            down(chip, piece_ref).wait_send()


def mesh_sems(lines, chips):
    return [
        pltpu.SemaphoreType.DMA,
        pltpu.SemaphoreType.DMA((chips,)),
        pltpu.SemaphoreType.DMA((chips,)),
        pltpu.SemaphoreType.DMA((lines, chips)),
        pltpu.SemaphoreType.DMA((lines, chips)),
        pltpu.SemaphoreType.DMA((lines, 2 * chips)),
    ]


def start_kernel(piece_ref, parts_ref, whole_ref, swapped_ref, *sems):
    greet_all(True)
    together(
        gather_mesh(piece_ref, whole_ref, *sems[:6]),
        swap_line(True, parts_ref, swapped_ref, *sems[6:]),
    )


def gather_and_swap(piece, parts, seq_count, head_count, collective_id):
    rows, width = piece.shape
    chips = head_count // 2
    _, two, depth, units = parts.shape
    whole, swapped = pl.pallas_call(
        start_kernel,
        in_specs=[ANY, ANY],
        out_specs=[ANY, ANY],
        out_shape=[
            jax.ShapeDtypeStruct((seq_count, head_count, rows, width), piece.dtype),
            jax.ShapeDtypeStruct((two, head_count * depth, units), parts.dtype),
        ],
        scratch_shapes=mesh_sems(seq_count, chips) + swap_sems(head_count),
        compiler_params=pltpu.CompilerParams(
            collective_id=collective_id, has_side_effects=True
        ),
        cost_estimate=pl.CostEstimate(
            flops=0, transcendentals=0, bytes_accessed=parts.size * 80
        ),
        name="gather_and_swap",
    )(piece, parts)
    return whole.reshape(seq_count * head_count * rows, width), swapped


def finish_kernel(part_ref, parts_ref, out_ref, swapped_ref, *scratch):
    greet_all(False)
    together(
        reduce_line(part_ref, out_ref, *scratch[:11]),
        swap_line(False, parts_ref, swapped_ref, *scratch[11:]),
    )


def reduce_and_swap(part, parts, head_count, collective_id):
    group, width = part.shape
    rows = group // head_count
    chips = head_count // 2
    two, depth, units = parts.shape
    return pl.pallas_call(
        finish_kernel,
        in_specs=[ANY, ANY],
        out_specs=[pl.BlockSpec(memory_space=pltpu.VMEM), ANY],
        out_shape=[
            jax.ShapeDtypeStruct((rows, width), jnp.float32),
            jax.ShapeDtypeStruct((head_count, two, depth // head_count, units), parts.dtype),
        ],
        scratch_shapes=reduce_scratch(chips, rows, width) + swap_sems(head_count),
        compiler_params=pltpu.CompilerParams(
            collective_id=collective_id, has_side_effects=True, vmem_limit_bytes=48 * 1024 * 1024
        ),
        cost_estimate=pl.CostEstimate(
            flops=0, transcendentals=0, bytes_accessed=2 * head_count * rows * width * 30
        ),
        name="reduce_and_swap",
    )(part.reshape(head_count, rows, width), parts)


def feed_kernel(
    normed_ref, cot_ref, gu_ref, down_ref, nmlp_ref, out_ref, act_ref, ggate_ref, gup_ref
):
    pieces, _, depth, _ = gu_ref.shape
    normed = normed_ref[...]
    gate = matmul(normed[:, :depth], gu_ref[0, 0])
    up = matmul(normed[:, :depth], gu_ref[0, 1])
    for s in range(1, pieces):
        part = normed[:, s * depth : (s + 1) * depth]
        gate += matmul(part, gu_ref[s, 0])
        up += matmul(part, gu_ref[s, 1])
    grad_act = contract(cot_ref[...], down_ref[...])
    sigmoid = 1.0 / (1.0 + jnp.exp(-gate))
    silu = gate * sigmoid
    activated = (silu * up).astype(jnp.bfloat16)
    act_ref[...] = activated
    grad_gate = (grad_act * up * (sigmoid * (1.0 + gate * (1.0 - sigmoid)))).astype(jnp.bfloat16)
    grad_up = (grad_act * silu).astype(jnp.bfloat16)
    ggate_ref[...] = grad_gate
    gup_ref[...] = grad_up
    for s in range(pieces):
        back = contract(grad_gate, gu_ref[s, 0]) + contract(grad_up, gu_ref[s, 1])
        nmlp_ref[:, s * depth : (s + 1) * depth] = back.astype(jnp.bfloat16)
    out_ref[...] = matmul(activated, down_ref[...]).astype(jnp.bfloat16)


def feed_forward(normed, cot, weight_gu, weight_down, block):
    group, model = normed.shape
    units = weight_down.shape[0]

    def rowed(cols):
        return pl.BlockSpec((block, cols), lambda i: (i, 0))

    return pl.pallas_call(
        feed_kernel,
        grid=(group // block,),
        in_specs=[
            rowed(model),
            rowed(model),
            pl.BlockSpec(weight_gu.shape, lambda i: (0, 0, 0, 0), pipeline_mode=pl.Buffered(1)),
            pl.BlockSpec(weight_down.shape, lambda i: (0, 0), pipeline_mode=pl.Buffered(1)),
        ],
        out_specs=[rowed(model), rowed(model), rowed(units), rowed(units), rowed(units)],
        out_shape=[
            jax.ShapeDtypeStruct((group, model), jnp.bfloat16),
            jax.ShapeDtypeStruct((group, model), jnp.bfloat16),
            jax.ShapeDtypeStruct((group, units), jnp.bfloat16),
            jax.ShapeDtypeStruct((group, units), jnp.bfloat16),
            jax.ShapeDtypeStruct((group, units), jnp.bfloat16),
        ],
        compiler_params=pltpu.CompilerParams(
            dimension_semantics=("arbitrary",), vmem_limit_bytes=56 * 1024 * 1024
        ),
        cost_estimate=pl.CostEstimate(
            flops=12 * group * model * units,
            transcendentals=group * units,
            bytes_accessed=2 * (4 * group * model + 3 * group * units + 3 * model * units),
        ),
        name="feed_forward",
    )(normed, cot, weight_gu, weight_down)


def weights_kernel(left_ref, right_ref, out_ref):
    product = transposed(left_ref[...], right_ref[...])
    out_ref[...] = product.astype(jnp.bfloat16).reshape(out_ref.shape)


def weight_product(left, right, rows, cols, out_shape, out_block, out_map, height=None):
    tokens = left.shape[0]
    height = height or left.shape[1]
    width = right.shape[1]
    return pl.pallas_call(
        weights_kernel,
        grid=(height // rows, width // cols),
        in_specs=[
            pl.BlockSpec((tokens, rows), lambda i, j: (0, i)),
            pl.BlockSpec((tokens, cols), lambda i, j: (0, j)),
        ],
        out_specs=pl.BlockSpec(out_block, out_map),
        out_shape=jax.ShapeDtypeStruct(out_shape, jnp.bfloat16),
        compiler_params=pltpu.CompilerParams(
            dimension_semantics=("arbitrary", "arbitrary"), vmem_limit_bytes=40 * 1024 * 1024
        ),
        cost_estimate=pl.CostEstimate(
            flops=2 * tokens * height * width,
            transcendentals=0,
            bytes_accessed=2 * (tokens * (height + width) + height * width),
        ),
        name="weight_product",
    )(left, right)


def packed_kernel(left_ref, right_ref, gains_ref, out_ref):
    cols = right_ref.shape[1]
    out_ref[:, :cols] = transposed(left_ref[...], right_ref[...]).astype(jnp.bfloat16)
    out_ref[:, cols:] = gains_ref[...]


def packed_product(left, right, gains, rows):
    tokens, model = left.shape
    cols = right.shape[1]
    width = cols + gains.shape[1]
    return pl.pallas_call(
        packed_kernel,
        grid=(model // rows,),
        in_specs=[
            pl.BlockSpec((tokens, rows), lambda i: (0, i)),
            pl.BlockSpec((tokens, cols), lambda i: (0, 0)),
            pl.BlockSpec((rows, gains.shape[1]), lambda i: (i, 0)),
        ],
        out_specs=pl.BlockSpec((rows, width), lambda i: (i, 0)),
        out_shape=jax.ShapeDtypeStruct((model, width), jnp.bfloat16),
        compiler_params=pltpu.CompilerParams(
            dimension_semantics=("arbitrary",), vmem_limit_bytes=32 * 1024 * 1024
        ),
        cost_estimate=pl.CostEstimate(
            flops=2 * tokens * model * cols,
            transcendentals=0,
            bytes_accessed=2 * (left.size + right.size + model * width),
        ),
        name="packed_product",
    )(left, right, gains)


def gu_kernel(left_ref, gate_ref, up_ref, out_ref):
    left = left_ref[...]
    out_ref[0, 0] = transposed(left, gate_ref[...]).astype(jnp.bfloat16)
    out_ref[0, 1] = transposed(left, up_ref[...]).astype(jnp.bfloat16)


def gu_product(normed, grad_gate, grad_up, pieces, split):
    tokens, model = normed.shape
    units = grad_gate.shape[1]
    depth = model // pieces
    rows = depth // split
    return pl.pallas_call(
        gu_kernel,
        grid=(pieces, split),
        in_specs=[
            pl.BlockSpec((tokens, rows), lambda s, i: (0, s * split + i)),
            pl.BlockSpec((tokens, units), lambda s, i: (0, 0), pipeline_mode=pl.Buffered(1)),
            pl.BlockSpec((tokens, units), lambda s, i: (0, 0), pipeline_mode=pl.Buffered(1)),
        ],
        out_specs=pl.BlockSpec((1, 2, rows, units), lambda s, i: (s, 0, i, 0)),
        out_shape=jax.ShapeDtypeStruct((pieces, 2, depth, units), jnp.bfloat16),
        compiler_params=pltpu.CompilerParams(
            dimension_semantics=("arbitrary", "arbitrary"), vmem_limit_bytes=40 * 1024 * 1024
        ),
        cost_estimate=pl.CostEstimate(
            flops=4 * tokens * model * units,
            transcendentals=0,
            bytes_accessed=2 * (normed.size + 2 * grad_gate.size + 2 * model * units),
        ),
        name="gu_product",
    )(normed, grad_gate, grad_up)


def shards(
    inputs,
    segments,
    cotangent,
    norm_attn,
    attn_in,
    norm_latent,
    query_up,
    out_proj,
    norm_mlp,
    gate_up,
    down_proj,
):
    head_count = lax.axis_size("head")
    head_place = lax.axis_index("head")
    shard_rows, model = inputs.shape
    group_rows = shard_rows * head_count
    block_rows = min(512, group_rows)
    seq_count = lax.axis_size("seq")
    own_rows = attn_in.shape[0]
    own_latent = norm_latent.shape[0]
    own_units = down_proj.shape[0]
    units = seq_count * own_units
    padded = -(-units // 128) * 128
    device_count = seq_count * head_count
    proj_cols = attn_in.shape[1]
    gain_cols = jnp.stack(
        [norm_attn, norm_mlp, jnp.pad(norm_latent, (0, own_rows - own_latent))], axis=1
    )
    packed = jnp.concatenate([attn_in, jnp.pad(gain_cols, ((0, 0), (0, 125)))], axis=1)
    pieces = gate_up.reshape(own_rows, 2, seq_count, head_count, own_units)
    pieces = pieces.transpose(3, 1, 0, 2, 4).reshape(head_count, 2, own_rows, units)
    pieces = jnp.pad(pieces, ((0, 0), (0, 0), (0, 0), (0, padded - units)))
    cot_all = lax.all_gather(cotangent, "head", axis=0, tiled=True)
    packed_all, turned = gather_and_swap(packed, pieces, seq_count, head_count, 0)
    weight_gu = lax.all_gather(turned[None], "seq", axis=0, tiled=True)
    weight_down = lax.all_gather(down_proj, "seq", axis=0, tiled=True)
    weight_down = jnp.pad(weight_down, ((0, padded - units), (0, 0)))
    weight_in = packed_all[:, :proj_cols]
    gain_attn = packed_all[:, proj_cols].astype(jnp.float32)
    gain_mlp = packed_all[:, proj_cols + 1].astype(jnp.float32)
    gain_latent = (
        packed_all[:, proj_cols + 2]
        .reshape(device_count, own_rows)[:, :own_latent]
        .reshape(device_count * own_latent)
        .astype(jnp.float32)
    )
    starts = segment_starts(segments[0])
    first_keys = starts[::block_rows] // block_rows
    cosine, sine = angles(starts)
    row_start = head_place * shard_rows
    cos_local = lax.dynamic_slice_in_dim(cosine, row_start, shard_rows, 0)
    sin_local = lax.dynamic_slice_in_dim(sine, row_start, shard_rows, 0)
    inputs_f = inputs.astype(jnp.float32)
    normed = rms_norm(inputs_f, gain_attn).astype(jnp.bfloat16)
    projected = jnp.dot(normed, weight_in, preferred_element_type=jnp.float32)
    latent = projected[:, :QR]
    key_raw = projected[:, QR : QR + DH]
    latent_n = rms_norm(latent, gain_latent).astype(jnp.bfloat16)
    keys_local = rotary(key_raw, cos_local, sin_local).astype(jnp.bfloat16)
    values_local = projected[:, QR + DH :].astype(jnp.bfloat16)
    joined_all = gather_head(
        tie(jnp.concatenate([latent_n, keys_local, values_local], axis=1), cot_all),
        head_count,
        1,
    )
    attn_part, queries, mixed, stats = attention_forward(
        joined_all, starts[:, None], cosine, sine, query_up, out_proj, first_keys, block_rows
    )
    attn_out = reduce_head(attn_part, head_count, 2)
    hidden = inputs_f + attn_out
    normed_mlp = rms_norm(hidden, gain_mlp).astype(jnp.bfloat16)
    nmlp_all = gather_head(tie(normed_mlp, weight_gu, weight_down), head_count, 3)
    nmlp_part, down_part, activated, grad_gate, grad_up = feed_forward(
        nmlp_all, cot_all, weight_gu, weight_down, 256
    )
    grad_nmlp = reduce_head(nmlp_part, head_count, 4)
    gu_part = gu_product(nmlp_all, grad_gate, grad_up, seq_count, 2)
    down_grad = weight_product(
        activated[:, :units],
        cot_all,
        units,
        512,
        (seq_count, own_units, model),
        (seq_count, own_units, 512),
        lambda i, j: (0, 0, j),
    )
    gu_rows = lax.psum_scatter(gu_part, "seq", scatter_dimension=0, tiled=True)
    down_rows = lax.psum_scatter(down_grad, "seq", scatter_dimension=0, tiled=True)
    norm_value, mlp_back = jax.vjp(rms_norm, hidden, gain_mlp)
    grad_hidden_n, mlpnorm_part = mlp_back(grad_nmlp)
    grad_hidden = cotangent.astype(jnp.float32) + grad_hidden_n
    grad_attn = grad_hidden.astype(jnp.bfloat16)
    grad_attn_all = gather_head(tie(grad_attn, gu_part, down_grad), head_count, 5)
    grad_part, grad_query = attention_backward(
        joined_all,
        starts[:, None],
        cosine,
        sine,
        query_up,
        out_proj,
        queries,
        mixed,
        stats,
        grad_attn_all,
        first_keys,
        block_rows,
    )
    received = reduce_head(grad_part, head_count, 6)
    head_cols = query_up.shape[1]
    queryup_part = weight_product(
        joined_all,
        grad_query,
        QR // seq_count,
        head_cols,
        (seq_count, QR // seq_count, head_cols),
        (1, QR // seq_count, head_cols),
        lambda i, j: (i, 0, 0),
        height=QR,
    )
    outproj_part = weight_product(
        mixed,
        grad_attn_all,
        head_cols,
        model // seq_count,
        (seq_count, head_cols, model // seq_count),
        (1, head_cols, model // seq_count),
        lambda i, j: (j, 0, 0),
    )
    received = tie(received, queryup_part, outproj_part, gu_rows, down_rows)
    grad_latent_n, grad_keys, grad_values = (
        received[:, :QR],
        received[:, QR : QR + DH],
        received[:, QR + DH :],
    )
    downproj_grad = down_rows[0].astype(jnp.float32)
    queryup_grad = lax.psum_scatter(queryup_part, "seq", scatter_dimension=0, tiled=True)
    queryup_grad = queryup_grad[0].astype(jnp.float32)
    outproj_grad = lax.psum_scatter(outproj_part, "seq", scatter_dimension=0, tiled=True)
    outproj_grad = outproj_grad[0].astype(jnp.float32)
    latent_value, latent_back = jax.vjp(rms_norm, latent, gain_latent)
    grad_latent, latnorm_part = latent_back(grad_latent_n)
    turned_key, key_back = jax.vjp(lambda key_in: rotary(key_in, cos_local, sin_local), key_raw)
    (grad_key_raw,) = key_back(grad_keys)
    grad_proj = jnp.concatenate([grad_latent, grad_key_raw, grad_values], axis=1).astype(
        jnp.bfloat16
    )
    grad_normed = contract(grad_proj, weight_in)
    input_value, input_back = jax.vjp(rms_norm, inputs_f, gain_attn)
    grad_input_n, attnnorm_part = input_back(grad_normed)
    input_grad = grad_hidden + grad_input_n
    latent_col = jnp.pad(
        latnorm_part.reshape(device_count, own_latent), ((0, 0), (0, own_rows - own_latent))
    ).reshape(device_count * own_rows)
    gain_parts = jnp.stack([attnnorm_part, mlpnorm_part, latent_col], axis=1)
    gain_parts = jnp.pad(gain_parts, ((0, 0), (0, 125))).astype(jnp.bfloat16)
    packed_part = packed_product(normed, grad_proj, gain_parts, min(512, model))
    down_out, gu_back = reduce_and_swap(
        tie(down_part, packed_part), gu_rows[0], head_count, 7
    )
    layer_out = (hidden + down_out).astype(jnp.bfloat16)
    gateup_grad = (
        gu_back[..., :units]
        .reshape(head_count, 2, own_rows, seq_count, own_units)
        .transpose(2, 1, 3, 0, 4)
        .reshape(own_rows, 2 * device_count * own_units)
        .astype(jnp.float32)
    )
    packed_rows = lax.psum_scatter(packed_part, "seq", scatter_dimension=0, tiled=True)
    packed_grad = lax.psum_scatter(
        tie(packed_rows, down_out), "head", scatter_dimension=0, tiled=True
    ).astype(jnp.float32)
    attnin_grad = packed_grad[:, :proj_cols]
    attnnorm_grad = packed_grad[:, proj_cols]
    mlpnorm_grad = packed_grad[:, proj_cols + 1]
    latnorm_grad = packed_grad[:own_latent, proj_cols + 2]
    return (
        layer_out,
        input_grad,
        attnnorm_grad,
        attnin_grad,
        latnorm_grad,
        queryup_grad,
        outproj_grad,
        mlpnorm_grad,
        gateup_grad,
        downproj_grad,
    )


def solution(mesh):
    in_specs = (
        P(("seq", "head"), None),
        P("seq", None),
        P(("seq", "head"), None),
        P(("seq", "head")),
        P(("seq", "head"), None),
        P(("seq", "head")),
        P(None, "head"),
        P("head", None),
        P(("seq", "head")),
        P(("seq", "head"), None),
        P(("seq", "head"), None),
    )
    out_specs = (
        P(("seq", "head"), None),
        P(("seq", "head"), None),
        P(("seq", "head")),
        P(("seq", "head"), None),
        P(("seq", "head")),
        P("seq", "head"),
        P("head", "seq"),
        P(("seq", "head")),
        P(("seq", "head"), None),
        P(("seq", "head"), None),
    )
    return jax.shard_map(shards, mesh=mesh, in_specs=in_specs, out_specs=out_specs, check_vma=False)
```

```python
import functools

import jax
import jax.numpy as jnp
from jax import lax
from jax.experimental import pallas as pl
from jax.experimental.pallas import tpu as pltpu
from jax.sharding import PartitionSpec as P

DH = 256
QR = 1024
HALF = DH // 2


EPS = 1e-06
THETA = 10000.0
NEG = -1e30


def contract(left, right):
    return lax.dot_general(
        left, right, (((1,), (1,)), ((), ())), preferred_element_type=jnp.float32
    )


def transposed(left, right):
    return lax.dot_general(
        left, right, (((0,), (0,)), ((), ())), preferred_element_type=jnp.float32
    )


def matmul(left, right):
    return jnp.dot(left, right, preferred_element_type=jnp.float32)


def rms_norm(values_in, gain_vec):
    return (
        values_in
        * lax.rsqrt(jnp.mean(values_in * values_in, axis=-1, keepdims=True) + EPS)
        * gain_vec
    )


def rotary(values_in, cosine, sine):
    half_dim = values_in.shape[-1] // 2
    first_half = values_in[..., :half_dim]
    second_half = values_in[..., half_dim:]
    return jnp.concatenate(
        [first_half * cosine - second_half * sine, second_half * cosine + first_half * sine],
        axis=-1,
    )


def segment_starts(segment_row):
    index = jnp.arange(segment_row.shape[0], dtype=jnp.int32)
    opens = jnp.concatenate([jnp.ones((1,), jnp.bool_), segment_row[1:] != segment_row[:-1]])
    return lax.cummax(jnp.where(opens, index, jnp.zeros_like(index)), axis=0)


def angles(starts):
    index = jnp.arange(starts.shape[0], dtype=jnp.int32)
    places = (index - starts).astype(jnp.float32)
    exponent = jnp.arange(DH // 2, dtype=jnp.float32) * (-2.0 / DH)
    frequency = jnp.power(jnp.float32(THETA), exponent)
    turned = places[:, None] * frequency[None, :]
    return (jnp.cos(turned), jnp.sin(turned))


def stacked(values_in, heads):
    return jnp.concatenate([values_in[:, h * DH : (h + 1) * DH] for h in range(heads)], axis=0)


def side_by_side(values_in, heads):
    rows = values_in.shape[0] // heads
    return jnp.concatenate([values_in[h * rows : (h + 1) * rows] for h in range(heads)], axis=1)


def block_mask(starts, query_row, key_row, heads, rows, cols):
    place_query = query_row + lax.broadcasted_iota(jnp.int32, (rows, cols), 0)
    place_key = key_row + lax.broadcasted_iota(jnp.int32, (rows, cols), 1)
    allowed = (place_key >= starts) & (place_key <= place_query)
    return jnp.concatenate([allowed] * heads, axis=0) if heads > 1 else allowed


def forward_kernel(
    heads,
    block,
    first_ref,
    joined_ref,
    starts_ref,
    cos_ref,
    sin_ref,
    queryup_ref,
    outproj_ref,
    part_ref,
    query_ref,
    mixed_ref,
    stats_ref,
    top_ref,
    total_ref,
    accum_ref,
):
    qblock = pl.program_id(0)
    query_row = pl.multiple_of(qblock * block, block)
    cosine = cos_ref[...]
    sine = sin_ref[...]
    raw = matmul(joined_ref[pl.ds(query_row, block), :QR], queryup_ref[...])
    turned = []
    for h in range(heads):
        one = raw[:, h * DH : h * DH + HALF]
        two = raw[:, h * DH + HALF : (h + 1) * DH]
        turned += [one * cosine - two * sine, two * cosine + one * sine]
    queries = (jnp.concatenate(turned, axis=1)).astype(jnp.bfloat16) * jnp.bfloat16(DH**-0.5)
    query_ref[...] = queries
    rows = stacked(queries, heads)
    starts = starts_ref[...]
    top_ref[...] = jnp.full_like(top_ref, NEG)
    total_ref[...] = jnp.zeros_like(total_ref)
    accum_ref[...] = jnp.zeros_like(accum_ref)

    def key_step(kblock, carry):
        key_row = pl.multiple_of(kblock * block, block)
        keys = joined_ref[pl.ds(key_row, block), QR : QR + DH]
        values = joined_ref[pl.ds(key_row, block), QR + DH :]
        scores = contract(rows, keys)
        allowed = block_mask(starts, query_row, key_row, heads, block, block)
        scores = jnp.where(allowed, scores, NEG)
        old_top = top_ref[...]
        new_top = jnp.maximum(old_top, jnp.max(scores, axis=1, keepdims=True))
        weights = jnp.exp(scores - new_top)
        shrink = jnp.exp(old_top - new_top)
        top_ref[...] = new_top
        total_ref[...] = total_ref[...] * shrink + jnp.sum(weights, axis=1, keepdims=True)
        accum_ref[...] = accum_ref[...] * shrink + matmul(weights.astype(jnp.bfloat16), values)
        return carry

    lax.fori_loop(first_ref[qblock], qblock + 1, key_step, 0)
    total = total_ref[...]
    mixed = side_by_side((accum_ref[...] / total).astype(jnp.bfloat16), heads)
    mixed_ref[...] = mixed
    stats_ref[...] = jnp.broadcast_to(top_ref[...] + jnp.log(total), (heads * block, 128))
    part_ref[...] = matmul(mixed, outproj_ref[...]).astype(jnp.bfloat16)


def attention_forward(joined, starts, cosine, sine, query_up, out_proj, first_keys, block):
    group, width = joined.shape
    heads = query_up.shape[1] // DH
    model = out_proj.shape[1]
    count = group // block

    def whole(shape):
        return pl.BlockSpec(shape, lambda i, first: (0, 0), pipeline_mode=pl.Buffered(1))

    def rowed(cols, rows=block):
        return pl.BlockSpec((rows, cols), lambda i, first: (i, 0))

    pairs = group * group * heads // 4
    return pl.pallas_call(
        functools.partial(forward_kernel, heads, block),
        grid_spec=pltpu.PrefetchScalarGridSpec(
            num_scalar_prefetch=1,
            grid=(count,),
            in_specs=[
                whole((group, width)),
                rowed(1),
                rowed(HALF),
                rowed(HALF),
                whole(query_up.shape),
                whole(out_proj.shape),
            ],
            out_specs=[
                rowed(model),
                rowed(heads * DH),
                rowed(heads * DH),
                rowed(128, heads * block),
            ],
            scratch_shapes=[
                pltpu.VMEM((heads * block, 1), jnp.float32),
                pltpu.VMEM((heads * block, 1), jnp.float32),
                pltpu.VMEM((heads * block, DH), jnp.float32),
            ],
        ),
        out_shape=[
            jax.ShapeDtypeStruct((group, model), jnp.bfloat16),
            jax.ShapeDtypeStruct((group, heads * DH), jnp.bfloat16),
            jax.ShapeDtypeStruct((group, heads * DH), jnp.bfloat16),
            jax.ShapeDtypeStruct((group * heads, 128), jnp.float32),
        ],
        compiler_params=pltpu.CompilerParams(
            dimension_semantics=("arbitrary",), vmem_limit_bytes=48 * 1024 * 1024
        ),
        cost_estimate=pl.CostEstimate(
            flops=2 * group * heads * DH * (QR + model) + 4 * pairs * DH,
            transcendentals=pairs,
            bytes_accessed=2 * (joined.size + query_up.size + out_proj.size)
            + 2 * group * (model + 2 * heads * DH)
            + 4 * group * heads * 128
            + 8 * group * HALF,
        ),
        name="attention_forward",
    )(first_keys, joined, starts, cosine, sine, query_up, out_proj)


def backward_kernel(
    heads,
    block,
    first_ref,
    joined_ref,
    starts_ref,
    cos_ref,
    sin_ref,
    queryup_ref,
    outproj_ref,
    query_ref,
    mixed_ref,
    stats_ref,
    grad_ref,
    part_ref,
    gradq_ref,
    keyacc_ref,
    valueacc_ref,
    accum_ref,
):
    qblock = pl.program_id(0)
    query_row = pl.multiple_of(qblock * block, block)

    @pl.when(qblock == 0)
    def _():
        keyacc_ref[...] = jnp.zeros_like(keyacc_ref)
        valueacc_ref[...] = jnp.zeros_like(valueacc_ref)

    grad_mixed = contract(grad_ref[...], outproj_ref[...]).astype(jnp.bfloat16)
    products = grad_mixed.astype(jnp.float32) * mixed_ref[...].astype(jnp.float32)
    dots = jnp.sum(stacked(products, heads), axis=1, keepdims=True)
    grads = stacked(grad_mixed, heads)
    rows = stacked(query_ref[...], heads)
    level = stats_ref[:, 0:1]
    starts = starts_ref[...]
    accum_ref[...] = jnp.zeros_like(accum_ref)

    def key_step(kblock, carry):
        key_row = pl.multiple_of(kblock * block, block)
        keys = joined_ref[pl.ds(key_row, block), QR : QR + DH]
        values = joined_ref[pl.ds(key_row, block), QR + DH :]
        scores = contract(rows, keys)
        allowed = block_mask(starts, query_row, key_row, heads, block, block)
        weights = jnp.exp(jnp.where(allowed, scores, NEG) - level)
        grad_weights = contract(grads, values)
        grad_scores = (weights * (grad_weights - dots)).astype(jnp.bfloat16)
        accum_ref[...] += matmul(grad_scores, keys)
        keyacc_ref[pl.ds(key_row, block), :] += transposed(grad_scores, rows)
        valueacc_ref[pl.ds(key_row, block), :] += transposed(weights.astype(jnp.bfloat16), grads)
        return carry

    lax.fori_loop(first_ref[qblock], qblock + 1, key_step, 0)
    cosine = cos_ref[...]
    sine = sin_ref[...]
    grad_turned = side_by_side(accum_ref[...] * DH**-0.5, heads)
    back = []
    for h in range(heads):
        one = grad_turned[:, h * DH : h * DH + HALF]
        two = grad_turned[:, h * DH + HALF : (h + 1) * DH]
        back += [one * cosine + two * sine, two * cosine - one * sine]
    grad_query = jnp.concatenate(back, axis=1).astype(jnp.bfloat16)
    gradq_ref[...] = grad_query
    part_ref[pl.ds(query_row, block), :QR] = contract(grad_query, queryup_ref[...]).astype(
        jnp.bfloat16
    )

    @pl.when(qblock == pl.num_programs(0) - 1)
    def _():
        part_ref[:, QR : QR + DH] = keyacc_ref[...].astype(jnp.bfloat16)
        part_ref[:, QR + DH :] = valueacc_ref[...].astype(jnp.bfloat16)


def attention_backward(
    joined, starts, cosine, sine, query_up, out_proj, queries, mixed, stats, grads, first_keys, block
):
    group, width = joined.shape
    heads = query_up.shape[1] // DH
    model = out_proj.shape[1]
    count = group // block

    def whole(shape):
        return pl.BlockSpec(shape, lambda i, first: (0, 0), pipeline_mode=pl.Buffered(1))

    def rowed(cols, rows=block):
        return pl.BlockSpec((rows, cols), lambda i, first: (i, 0))

    pairs = group * group * heads // 4
    return pl.pallas_call(
        functools.partial(backward_kernel, heads, block),
        grid_spec=pltpu.PrefetchScalarGridSpec(
            num_scalar_prefetch=1,
            grid=(count,),
            in_specs=[
                whole((group, width)),
                rowed(1),
                rowed(HALF),
                rowed(HALF),
                whole(query_up.shape),
                whole(out_proj.shape),
                rowed(heads * DH),
                rowed(heads * DH),
                rowed(128, heads * block),
                rowed(model),
            ],
            out_specs=[
                pl.BlockSpec((group, width), lambda i, first: (0, 0)),
                rowed(heads * DH),
            ],
            scratch_shapes=[
                pltpu.VMEM((group, DH), jnp.float32),
                pltpu.VMEM((group, DH), jnp.float32),
                pltpu.VMEM((heads * block, DH), jnp.float32),
            ],
        ),
        out_shape=[
            jax.ShapeDtypeStruct((group, width), jnp.bfloat16),
            jax.ShapeDtypeStruct((group, heads * DH), jnp.bfloat16),
        ],
        compiler_params=pltpu.CompilerParams(
            dimension_semantics=("arbitrary",), vmem_limit_bytes=56 * 1024 * 1024
        ),
        cost_estimate=pl.CostEstimate(
            flops=2 * group * heads * DH * (QR + model) + 10 * pairs * DH,
            transcendentals=pairs,
            bytes_accessed=2 * (2 * joined.size + query_up.size + out_proj.size)
            + 2 * group * (model + 3 * heads * DH)
            + 4 * group * heads * 128
            + 8 * group * HALF,
        ),
        name="attention_backward",
    )(
        first_keys,
        joined,
        starts,
        cosine,
        sine,
        query_up,
        out_proj,
        queries,
        mixed,
        stats,
        grads,
    )


def tie(value, *others):
    return lax.optimization_barrier((value,) + others)[0]


MESH = pl.DeviceIdType.MESH
ANY = pl.BlockSpec(memory_space=pl.ANY)


def send(source, target, send_sem, recv_sem, place):
    return pltpu.make_async_remote_copy(
        src_ref=source,
        dst_ref=target,
        send_sem=send_sem,
        recv_sem=recv_sem,
        device_id={"head": place},
        device_id_type=MESH,
    )


def greet(place, spot, chips, sibling):
    barrier = pltpu.get_barrier_semaphore()
    pl.semaphore_signal(barrier, inc=1, device_id={"head": sibling}, device_id_type=MESH)

    @pl.when(spot > 0)
    def _():
        pl.semaphore_signal(barrier, inc=1, device_id={"head": place - 2}, device_id_type=MESH)

    @pl.when(spot < chips - 1)
    def _():
        pl.semaphore_signal(barrier, inc=1, device_id={"head": place + 2}, device_id_type=MESH)

    below = (spot + chips - 1) // chips
    above = (2 * chips - 2 - spot) // chips
    pl.semaphore_wait(barrier, 1 + below + above)


def line_places():
    place = lax.axis_index("head")
    chips = lax.axis_size("head") // 2
    spot = place // 2
    core = lax.rem(place, 2)
    return place, chips, spot, core, place + 1 - 2 * core


CUTS = 4


def gather_line(piece_ref, whole_ref, local_sem, up_sem, down_sem, side_sem, recv_sem):
    place, chips, spot, core, sibling = line_places()
    rows = piece_ref.shape[0] // CUTS

    def slot(chip, which, cut):
        return whole_ref.at[2 * chip + which, pl.ds(cut * rows, rows)]

    def mine(cut):
        return piece_ref.at[pl.ds(cut * rows, rows)]

    def up(chip, cut, source):
        received = recv_sem.at[2 * chip + core, cut]
        return send(source, slot(chip, core, cut), up_sem.at[chip, cut], received, place + 2)

    def down(chip, cut, source):
        received = recv_sem.at[2 * chip + core, cut]
        return send(source, slot(chip, core, cut), down_sem.at[chip, cut], received, place - 2)

    def side(chip, cut, source):
        received = recv_sem.at[2 * chip + core, cut]
        return send(source, slot(chip, core, cut), side_sem.at[chip, cut], received, sibling)

    own = pltpu.make_async_copy(piece_ref, whole_ref.at[place], local_sem)
    for cut in range(CUTS):

        @pl.when(spot < chips - 1)
        def _():
            up(spot, cut, mine(cut)).start()

        @pl.when(spot > 0)
        def _():
            down(spot, cut, mine(cut)).start()

    for cut in range(CUTS):
        side(spot, cut, mine(cut)).start()
    own.start()
    yield

    for k in range(1, chips):
        below = spot - k
        above = spot + k
        for cut in range(CUTS):

            @pl.when(below >= 0)
            def _():
                landed = slot(below, core, cut)
                up(below, cut, landed).wait_recv()

                @pl.when(spot < chips - 1)
                def _():
                    up(below, cut, landed).start()

                side(below, cut, landed).start()

            @pl.when(above < chips)
            def _():
                landed = slot(above, core, cut)
                down(above, cut, landed).wait_recv()

                @pl.when(spot > 0)
                def _():
                    down(above, cut, landed).start()

                side(above, cut, landed).start()

            yield

    own.wait()
    for chip in range(chips):
        for cut in range(CUTS):
            received = recv_sem.at[2 * chip + 1 - core, cut]
            send(
                mine(cut), slot(chip, 1 - core, cut), side_sem.at[chip, cut], received, sibling
            ).wait_recv()
            side(chip, cut, mine(cut)).wait_send()

            @pl.when((chip <= spot) & (spot < chips - 1))
            def _():
                up(chip, cut, mine(cut)).wait_send()

            @pl.when((chip >= spot) & (spot > 0))
            def _():
                down(chip, cut, mine(cut)).wait_send()


def together(*lines):
    active = list(lines)
    while active:
        active = [line for line in active if next(line, active) is None]


def gather_sems(chips):
    return [
        pltpu.SemaphoreType.DMA,
        pltpu.SemaphoreType.DMA((chips, CUTS)),
        pltpu.SemaphoreType.DMA((chips, CUTS)),
        pltpu.SemaphoreType.DMA((chips, CUTS)),
        pltpu.SemaphoreType.DMA((2 * chips, CUTS)),
    ]


def gather_kernel(piece_ref, whole_ref, *sems):
    place, chips, spot, core, sibling = line_places()
    greet(place, spot, chips, sibling)
    together(gather_line(piece_ref, whole_ref, *sems))


def gather_head(piece, head_count, collective_id):
    rows, width = piece.shape
    chips = head_count // 2
    whole = pl.pallas_call(
        gather_kernel,
        in_specs=[ANY],
        out_specs=ANY,
        out_shape=jax.ShapeDtypeStruct((head_count, rows, width), piece.dtype),
        scratch_shapes=gather_sems(chips),
        compiler_params=pltpu.CompilerParams(
            collective_id=collective_id, has_side_effects=True
        ),
        cost_estimate=pl.CostEstimate(
            flops=0, transcendentals=0, bytes_accessed=2 * head_count * rows * width * 20
        ),
        name="gather_head",
    )(piece)
    return whole.reshape(head_count * rows, width)


def reduce_line(
    part_ref,
    out_ref,
    own_buf,
    side_buf,
    below_buf,
    above_buf,
    load_sem,
    side_send,
    side_recv,
    up_send,
    up_recv,
    down_send,
    down_recv,
):
    place, chips, spot, core, sibling = line_places()
    rows = own_buf.shape[1] // CUTS

    def cut_of(ref, chip, cut):
        return ref.at[chip, pl.ds(cut * rows, rows)]

    def side(chip, cut):
        return send(
            cut_of(part_ref, 2 * chip + 1 - core, cut),
            cut_of(side_buf, chip, cut),
            side_send.at[chip, cut],
            side_recv.at[chip, cut],
            sibling,
        )

    def load(chip, cut):
        return pltpu.make_async_copy(
            cut_of(part_ref, 2 * chip + core, cut),
            cut_of(own_buf, chip, cut),
            load_sem.at[chip, cut],
        )

    def up(chip, cut):
        return send(
            cut_of(own_buf, chip, cut),
            cut_of(below_buf, chip, cut),
            up_send.at[chip, cut],
            up_recv.at[chip, cut],
            place + 2,
        )

    def down(chip, cut):
        return send(
            cut_of(own_buf, chip, cut),
            cut_of(above_buf, chip, cut),
            down_send.at[chip, cut],
            down_recv.at[chip, cut],
            place - 2,
        )

    order = []
    for k in range((chips + 1) // 2):
        order += [k] if k == chips - 1 - k else [chips - 1 - k, k]
    for chip in order:
        for cut in range(CUTS):
            side(chip, cut).start()
            load(chip, cut).start()
    yield

    def add(chip, cut, others, target):
        @pl.loop(0, rows // 16)
        def _(i):
            part = pl.ds(pl.multiple_of(cut * rows + i * 16, 16), 16)
            total = own_buf[chip, part, :].astype(jnp.float32)
            for other in others:
                total += other[chip, part, :].astype(jnp.float32)
            if target is None:
                own_buf[chip, part, :] = total.astype(own_buf.dtype)
            else:
                target[part, :] = total.astype(target.dtype)

    def ready(chip, cut):
        side(chip, cut).wait_recv()
        load(chip, cut).wait()

    for k in range(chips - 1):
        high = chips - 1 - k
        low = k
        for cut in range(CUTS):

            @pl.when(spot < high)
            def _():
                ready(high, cut)

                @pl.when(spot > 0)
                def _():
                    up(high, cut).wait_recv()
                    add(high, cut, [side_buf, below_buf], None)

                @pl.when(spot == 0)
                def _():
                    add(high, cut, [side_buf], None)

                up(high, cut).start()

            @pl.when(spot > low)
            def _():
                ready(low, cut)

                @pl.when(spot < chips - 1)
                def _():
                    down(low, cut).wait_recv()
                    add(low, cut, [side_buf, above_buf], None)

                @pl.when(spot == chips - 1)
                def _():
                    add(low, cut, [side_buf], None)

                down(low, cut).start()

            yield

    for chip in range(chips):

        @pl.when(spot == chip)
        def _():
            for cut in range(CUTS):
                ready(chip, cut)
                others = [side_buf]
                if chip > 0:
                    up(chip, cut).wait_recv()
                    others.append(below_buf)
                if chip < chips - 1:
                    down(chip, cut).wait_recv()
                    others.append(above_buf)
                add(chip, cut, others, out_ref)

        for cut in range(CUTS):
            side(chip, cut).wait_send()

            @pl.when(spot < chip)
            def _():
                up(chip, cut).wait_send()

            @pl.when(spot > chip)
            def _():
                down(chip, cut).wait_send()


def reduce_scratch(chips, rows, width):
    return [pltpu.VMEM((chips, rows, width), jnp.bfloat16)] * 4 + [
        pltpu.SemaphoreType.DMA((chips, CUTS))
    ] * 7


def reduce_kernel(part_ref, out_ref, *scratch):
    place, chips, spot, core, sibling = line_places()
    greet(place, spot, chips, sibling)
    together(reduce_line(part_ref, out_ref, *scratch))


def reduce_head(part, head_count, collective_id):
    group, width = part.shape
    rows = group // head_count
    chips = head_count // 2
    return pl.pallas_call(
        reduce_kernel,
        in_specs=[ANY],
        out_specs=pl.BlockSpec(memory_space=pltpu.VMEM),
        out_shape=jax.ShapeDtypeStruct((rows, width), jnp.float32),
        scratch_shapes=reduce_scratch(chips, rows, width),
        compiler_params=pltpu.CompilerParams(
            collective_id=collective_id, has_side_effects=True, vmem_limit_bytes=48 * 1024 * 1024
        ),
        cost_estimate=pl.CostEstimate(
            flops=0, transcendentals=0, bytes_accessed=2 * head_count * rows * width * 20
        ),
        name="reduce_head",
    )(part.reshape(head_count, rows, width))


def greet_all(with_lines):
    barrier = pltpu.get_barrier_semaphore()
    waits = 0
    for axis in ("head", "seq") if with_lines else ("head",):
        own = lax.axis_index(axis)
        count = lax.axis_size(axis)
        for shift in range(1, count):
            peer = lax.rem(own + shift, count)
            pl.semaphore_signal(barrier, inc=1, device_id={axis: peer}, device_id_type=MESH)
        waits += count - 1
    pl.semaphore_wait(barrier, waits)


def swap_line(scatter, piece_ref, out_ref, local_sem, send_sem, recv_sem):
    place = lax.axis_index("head")
    count = lax.axis_size("head")
    rows = piece_ref.shape[2] if scatter else piece_ref.shape[1] // count

    def source(index):
        if scatter:
            return piece_ref.at[index]
        return piece_ref.at[:, pl.ds(pl.multiple_of(index * rows, rows), rows), :]

    def target(index):
        if scatter:
            return out_ref.at[:, pl.ds(pl.multiple_of(index * rows, rows), rows), :]
        return out_ref.at[index]

    own = pltpu.make_async_copy(source(place), target(place), local_sem)
    own.start()
    copies = []
    for shift in range(1, count):
        peer = lax.rem(place + shift, count)
        copy = send(
            source(peer), target(place), send_sem.at[shift], recv_sem.at[shift], peer
        )
        copy.start()
        copies.append(copy)
    yield
    own.wait()
    for copy in copies:
        copy.wait()


def swap_sems(count):
    return [
        pltpu.SemaphoreType.DMA,
        pltpu.SemaphoreType.DMA((count,)),
        pltpu.SemaphoreType.DMA((count,)),
    ]


def gather_mesh(piece_ref, whole_ref, local_sem, up_sem, down_sem, seq_sem, side_sem, recv_sem):
    place, chips, spot, core, sibling = line_places()
    line = lax.axis_index("seq")
    lines = lax.axis_size("seq")

    def slot(row, chip, which):
        return whole_ref.at[row, 2 * chip + which]

    def to(axis, where, row, chip, source, sem):
        return pltpu.make_async_remote_copy(
            src_ref=source,
            dst_ref=slot(row, chip, core),
            send_sem=sem,
            recv_sem=recv_sem.at[row, 2 * chip + core],
            device_id={axis: where},
            device_id_type=MESH,
        )

    def up(chip, source):
        return to("head", place + 2, line, chip, source, up_sem.at[chip])

    def down(chip, source):
        return to("head", place - 2, line, chip, source, down_sem.at[chip])

    def across(shift, chip, source):
        where = lax.rem(line + shift, lines)
        return to("seq", where, line, chip, source, seq_sem.at[shift, chip])

    def side(row, chip, source):
        return to("head", sibling, row, chip, source, side_sem.at[row, chip])

    def spread(chip, source):
        for shift in range(1, lines):
            across(shift, chip, source).start()
        side(line, chip, source).start()

    own = pltpu.make_async_copy(piece_ref, slot(line, spot, core), local_sem)

    @pl.when(spot < chips - 1)
    def _():
        up(spot, piece_ref).start()

    @pl.when(spot > 0)
    def _():
        down(spot, piece_ref).start()

    spread(spot, piece_ref)
    own.start()
    yield

    for k in range(1, chips):
        below = spot - k
        above = spot + k

        @pl.when(below >= 0)
        def _():
            landed = slot(line, below, core)
            up(below, landed).wait_recv()

            @pl.when(spot < chips - 1)
            def _():
                up(below, landed).start()

            spread(below, landed)

        @pl.when(above < chips)
        def _():
            landed = slot(line, above, core)
            down(above, landed).wait_recv()

            @pl.when(spot > 0)
            def _():
                down(above, landed).start()

            spread(above, landed)

        yield

    for chip in range(chips):
        for shift in range(1, lines):
            row = lax.rem(line + shift, lines)
            landed = slot(row, chip, core)
            to("seq", row, row, chip, landed, seq_sem.at[shift, chip]).wait_recv()
            side(row, chip, landed).start()
        yield

    own.wait()
    for chip in range(chips):
        for row in range(lines):
            landed = slot(row, chip, 1 - core)
            pltpu.make_async_remote_copy(
                src_ref=landed,
                dst_ref=landed,
                send_sem=side_sem.at[row, chip],
                recv_sem=recv_sem.at[row, 2 * chip + 1 - core],
                device_id={"head": sibling},
                device_id_type=MESH,
            ).wait_recv()
            side(row, chip, piece_ref).wait_send()
        for shift in range(1, lines):
            across(shift, chip, piece_ref).wait_send()

        @pl.when((chip <= spot) & (spot < chips - 1))
        def _():
            up(chip, piece_ref).wait_send()

        @pl.when((chip >= spot) & (spot > 0))
        def _():
            down(chip, piece_ref).wait_send()


def mesh_sems(lines, chips):
    return [
        pltpu.SemaphoreType.DMA,
        pltpu.SemaphoreType.DMA((chips,)),
        pltpu.SemaphoreType.DMA((chips,)),
        pltpu.SemaphoreType.DMA((lines, chips)),
        pltpu.SemaphoreType.DMA((lines, chips)),
        pltpu.SemaphoreType.DMA((lines, 2 * chips)),
    ]


def start_kernel(piece_ref, parts_ref, whole_ref, swapped_ref, *sems):
    greet_all(True)
    together(
        gather_mesh(piece_ref, whole_ref, *sems[:6]),
        swap_line(True, parts_ref, swapped_ref, *sems[6:]),
    )


def gather_and_swap(piece, parts, seq_count, head_count, collective_id):
    rows, width = piece.shape
    chips = head_count // 2
    _, two, depth, units = parts.shape
    whole, swapped = pl.pallas_call(
        start_kernel,
        in_specs=[ANY, ANY],
        out_specs=[ANY, ANY],
        out_shape=[
            jax.ShapeDtypeStruct((seq_count, head_count, rows, width), piece.dtype),
            jax.ShapeDtypeStruct((two, head_count * depth, units), parts.dtype),
        ],
        scratch_shapes=mesh_sems(seq_count, chips) + swap_sems(head_count),
        compiler_params=pltpu.CompilerParams(
            collective_id=collective_id, has_side_effects=True
        ),
        cost_estimate=pl.CostEstimate(
            flops=0, transcendentals=0, bytes_accessed=parts.size * 80
        ),
        name="gather_and_swap",
    )(piece, parts)
    return whole.reshape(seq_count * head_count * rows, width), swapped


def reduce_mesh(
    part_ref,
    out_ref,
    own_buf,
    side_buf,
    across_buf,
    line_buf,
    below_buf,
    above_buf,
    load_sem,
    side_send,
    side_recv,
    across_send,
    across_recv,
    up_send,
    up_recv,
    down_send,
    down_recv,
):
    place, chips, spot, core, sibling = line_places()
    line = lax.axis_index("seq")
    lines = lax.axis_size("seq")
    rows = own_buf.shape[2]

    def row_of(shift):
        return lax.rem(line + shift, lines)

    def side(shift):
        row = row_of(shift)
        return send(
            part_ref.at[row, :, 1 - core],
            side_buf.at[row],
            side_send.at[row],
            side_recv.at[row],
            sibling,
        )

    def load(shift):
        row = row_of(shift)
        return pltpu.make_async_copy(part_ref.at[row, :, core], own_buf.at[row], load_sem.at[row])

    def across(shift, chip):
        return pltpu.make_async_remote_copy(
            src_ref=own_buf.at[row_of(shift), chip],
            dst_ref=across_buf.at[shift, chip],
            send_sem=across_send.at[shift, chip],
            recv_sem=across_recv.at[shift, chip],
            device_id={"seq": row_of(shift)},
            device_id_type=MESH,
        )

    def hop(chip, target, send_sem, recv_sem, where):
        return send(
            line_buf.at[chip], target.at[chip], send_sem.at[chip], recv_sem.at[chip], where
        )

    def up(chip):
        return hop(chip, below_buf, up_send, up_recv, place + 2)

    def down(chip):
        return hop(chip, above_buf, down_send, down_recv, place - 2)

    def add(terms, target):
        @pl.loop(0, rows // 16)
        def _(i):
            part = pl.ds(pl.multiple_of(i * 16, 16), 16)
            total = terms[0][part, :].astype(jnp.float32)
            for term in terms[1:]:
                total += term[part, :].astype(jnp.float32)
            target[part, :] = total.astype(target.dtype)

    order = []
    for k in range((chips + 1) // 2):
        order += [k] if k == chips - 1 - k else [chips - 1 - k, k]
    shifts = list(range(1, lines)) + [0]
    for shift in shifts:
        side(shift).start()
        load(shift).start()
    for shift in shifts:
        side(shift).wait_recv()
        load(shift).wait()
        row = row_of(shift)
        if shift:
            for chip in order:
                add([own_buf.at[row, chip], side_buf.at[row, chip]], own_buf.at[row, chip])
                across(shift, chip).start()
            yield

    for chip in order:
        for shift in range(1, lines):
            across(shift, chip).wait_recv()
        terms = [own_buf.at[line, chip], side_buf.at[line, chip]]
        terms += [across_buf.at[shift, chip] for shift in range(1, lines)]
        add(terms, line_buf.at[chip])

        if chip > 0:

            @pl.when(spot == 0)
            def _():
                up(chip).start()

        if chip < chips - 1:

            @pl.when(spot == chips - 1)
            def _():
                down(chip).start()

        yield

    for k in range(chips - 1):
        high = chips - 1 - k
        low = k

        @pl.when((spot < high) & (spot > 0))
        def _():
            up(high).wait_recv()
            add([line_buf.at[high], below_buf.at[high]], line_buf.at[high])
            up(high).start()

        @pl.when((spot > low) & (spot < chips - 1))
        def _():
            down(low).wait_recv()
            add([line_buf.at[low], above_buf.at[low]], line_buf.at[low])
            down(low).start()

        yield

    for chip in range(chips):

        @pl.when(spot == chip)
        def _():
            terms = [line_buf.at[chip]]
            if chip > 0:
                up(chip).wait_recv()
                terms.append(below_buf.at[chip])
            if chip < chips - 1:
                down(chip).wait_recv()
                terms.append(above_buf.at[chip])
            add(terms, out_ref)

        for shift in range(1, lines):
            across(shift, chip).wait_send()

        @pl.when(spot < chip)
        def _():
            up(chip).wait_send()

        @pl.when(spot > chip)
        def _():
            down(chip).wait_send()

    for shift in shifts:
        side(shift).wait_send()


def mesh_scratch(lines, chips, rows, width):
    whole = pltpu.VMEM((lines, chips, rows, width), jnp.bfloat16)
    line = pltpu.VMEM((chips, rows, width), jnp.bfloat16)
    per_line = pltpu.SemaphoreType.DMA((lines,))
    per_chip = pltpu.SemaphoreType.DMA((chips,))
    both = pltpu.SemaphoreType.DMA((lines, chips))
    return [whole] * 3 + [line] * 3 + [per_line] * 3 + [both] * 2 + [per_chip] * 4


def finish_kernel(
    packed_ref, part_ref, parts_ref, packed_out_ref, out_ref, swapped_ref, *scratch
):
    greet_all(True)
    together(
        reduce_mesh(packed_ref, packed_out_ref, *scratch[:15]),
        reduce_line(part_ref, out_ref, *scratch[15:26]),
        swap_line(False, parts_ref, swapped_ref, *scratch[26:]),
    )


def reduce_and_swap(packed, part, parts, seq_count, head_count, collective_id):
    group, width = part.shape
    rows = group // head_count
    chips = head_count // 2
    two, depth, units = parts.shape
    packed_rows = packed.shape[0] // (seq_count * head_count)
    packed_width = packed.shape[1]
    vmem = pl.BlockSpec(memory_space=pltpu.VMEM)
    return pl.pallas_call(
        finish_kernel,
        in_specs=[ANY, ANY, ANY],
        out_specs=[vmem, vmem, ANY],
        out_shape=[
            jax.ShapeDtypeStruct((packed_rows, packed_width), jnp.float32),
            jax.ShapeDtypeStruct((rows, width), jnp.float32),
            jax.ShapeDtypeStruct((head_count, two, depth // head_count, units), parts.dtype),
        ],
        scratch_shapes=mesh_scratch(seq_count, chips, packed_rows, packed_width)
        + reduce_scratch(chips, rows, width)
        + swap_sems(head_count),
        compiler_params=pltpu.CompilerParams(
            collective_id=collective_id, has_side_effects=True, vmem_limit_bytes=56 * 1024 * 1024
        ),
        cost_estimate=pl.CostEstimate(
            flops=0, transcendentals=0, bytes_accessed=2 * head_count * rows * width * 30
        ),
        name="reduce_and_swap",
    )(
        packed.reshape(seq_count, chips, 2, packed_rows, packed_width),
        part.reshape(head_count, rows, width),
        parts,
    )


def feed_kernel(
    normed_ref, cot_ref, gu_ref, down_ref, nmlp_ref, out_ref, act_ref, ggate_ref, gup_ref
):
    pieces, _, depth, _ = gu_ref.shape
    normed = normed_ref[...]
    gate = matmul(normed[:, :depth], gu_ref[0, 0])
    up = matmul(normed[:, :depth], gu_ref[0, 1])
    for s in range(1, pieces):
        part = normed[:, s * depth : (s + 1) * depth]
        gate += matmul(part, gu_ref[s, 0])
        up += matmul(part, gu_ref[s, 1])
    grad_act = contract(cot_ref[...], down_ref[...])
    sigmoid = 1.0 / (1.0 + jnp.exp(-gate))
    silu = gate * sigmoid
    activated = (silu * up).astype(jnp.bfloat16)
    act_ref[...] = activated
    grad_gate = (grad_act * up * (sigmoid * (1.0 + gate * (1.0 - sigmoid)))).astype(jnp.bfloat16)
    grad_up = (grad_act * silu).astype(jnp.bfloat16)
    ggate_ref[...] = grad_gate
    gup_ref[...] = grad_up
    for s in range(pieces):
        back = contract(grad_gate, gu_ref[s, 0]) + contract(grad_up, gu_ref[s, 1])
        nmlp_ref[:, s * depth : (s + 1) * depth] = back.astype(jnp.bfloat16)
    out_ref[...] = matmul(activated, down_ref[...]).astype(jnp.bfloat16)


def feed_forward(normed, cot, weight_gu, weight_down, block):
    group, model = normed.shape
    units = weight_down.shape[0]

    def rowed(cols):
        return pl.BlockSpec((block, cols), lambda i: (i, 0))

    return pl.pallas_call(
        feed_kernel,
        grid=(group // block,),
        in_specs=[
            rowed(model),
            rowed(model),
            pl.BlockSpec(weight_gu.shape, lambda i: (0, 0, 0, 0), pipeline_mode=pl.Buffered(1)),
            pl.BlockSpec(weight_down.shape, lambda i: (0, 0), pipeline_mode=pl.Buffered(1)),
        ],
        out_specs=[rowed(model), rowed(model), rowed(units), rowed(units), rowed(units)],
        out_shape=[
            jax.ShapeDtypeStruct((group, model), jnp.bfloat16),
            jax.ShapeDtypeStruct((group, model), jnp.bfloat16),
            jax.ShapeDtypeStruct((group, units), jnp.bfloat16),
            jax.ShapeDtypeStruct((group, units), jnp.bfloat16),
            jax.ShapeDtypeStruct((group, units), jnp.bfloat16),
        ],
        compiler_params=pltpu.CompilerParams(
            dimension_semantics=("arbitrary",), vmem_limit_bytes=56 * 1024 * 1024
        ),
        cost_estimate=pl.CostEstimate(
            flops=12 * group * model * units,
            transcendentals=group * units,
            bytes_accessed=2 * (4 * group * model + 3 * group * units + 3 * model * units),
        ),
        name="feed_forward",
    )(normed, cot, weight_gu, weight_down)


def weights_kernel(left_ref, right_ref, out_ref):
    product = transposed(left_ref[...], right_ref[...])
    out_ref[...] = product.astype(jnp.bfloat16).reshape(out_ref.shape)


def weight_product(left, right, rows, cols, out_shape, out_block, out_map, height=None):
    tokens = left.shape[0]
    height = height or left.shape[1]
    width = right.shape[1]
    return pl.pallas_call(
        weights_kernel,
        grid=(height // rows, width // cols),
        in_specs=[
            pl.BlockSpec((tokens, rows), lambda i, j: (0, i)),
            pl.BlockSpec((tokens, cols), lambda i, j: (0, j)),
        ],
        out_specs=pl.BlockSpec(out_block, out_map),
        out_shape=jax.ShapeDtypeStruct(out_shape, jnp.bfloat16),
        compiler_params=pltpu.CompilerParams(
            dimension_semantics=("arbitrary", "arbitrary"), vmem_limit_bytes=40 * 1024 * 1024
        ),
        cost_estimate=pl.CostEstimate(
            flops=2 * tokens * height * width,
            transcendentals=0,
            bytes_accessed=2 * (tokens * (height + width) + height * width),
        ),
        name="weight_product",
    )(left, right)


def packed_kernel(left_ref, right_ref, gains_ref, out_ref):
    cols = right_ref.shape[1]
    out_ref[:, :cols] = transposed(left_ref[...], right_ref[...]).astype(jnp.bfloat16)
    out_ref[:, cols:] = gains_ref[...]


def packed_product(left, right, gains, rows):
    tokens, model = left.shape
    cols = right.shape[1]
    width = cols + gains.shape[1]
    return pl.pallas_call(
        packed_kernel,
        grid=(model // rows,),
        in_specs=[
            pl.BlockSpec((tokens, rows), lambda i: (0, i)),
            pl.BlockSpec((tokens, cols), lambda i: (0, 0)),
            pl.BlockSpec((rows, gains.shape[1]), lambda i: (i, 0)),
        ],
        out_specs=pl.BlockSpec((rows, width), lambda i: (i, 0)),
        out_shape=jax.ShapeDtypeStruct((model, width), jnp.bfloat16),
        compiler_params=pltpu.CompilerParams(
            dimension_semantics=("arbitrary",), vmem_limit_bytes=32 * 1024 * 1024
        ),
        cost_estimate=pl.CostEstimate(
            flops=2 * tokens * model * cols,
            transcendentals=0,
            bytes_accessed=2 * (left.size + right.size + model * width),
        ),
        name="packed_product",
    )(left, right, gains)


def gu_kernel(left_ref, gate_ref, up_ref, out_ref):
    left = left_ref[...]
    out_ref[0, 0] = transposed(left, gate_ref[...]).astype(jnp.bfloat16)
    out_ref[0, 1] = transposed(left, up_ref[...]).astype(jnp.bfloat16)


def gu_product(normed, grad_gate, grad_up, pieces, split):
    tokens, model = normed.shape
    units = grad_gate.shape[1]
    depth = model // pieces
    rows = depth // split
    return pl.pallas_call(
        gu_kernel,
        grid=(pieces, split),
        in_specs=[
            pl.BlockSpec((tokens, rows), lambda s, i: (0, s * split + i)),
            pl.BlockSpec((tokens, units), lambda s, i: (0, 0), pipeline_mode=pl.Buffered(1)),
            pl.BlockSpec((tokens, units), lambda s, i: (0, 0), pipeline_mode=pl.Buffered(1)),
        ],
        out_specs=pl.BlockSpec((1, 2, rows, units), lambda s, i: (s, 0, i, 0)),
        out_shape=jax.ShapeDtypeStruct((pieces, 2, depth, units), jnp.bfloat16),
        compiler_params=pltpu.CompilerParams(
            dimension_semantics=("arbitrary", "arbitrary"), vmem_limit_bytes=40 * 1024 * 1024
        ),
        cost_estimate=pl.CostEstimate(
            flops=4 * tokens * model * units,
            transcendentals=0,
            bytes_accessed=2 * (normed.size + 2 * grad_gate.size + 2 * model * units),
        ),
        name="gu_product",
    )(normed, grad_gate, grad_up)


def shards(
    inputs,
    segments,
    cotangent,
    norm_attn,
    attn_in,
    norm_latent,
    query_up,
    out_proj,
    norm_mlp,
    gate_up,
    down_proj,
):
    head_count = lax.axis_size("head")
    head_place = lax.axis_index("head")
    shard_rows, model = inputs.shape
    group_rows = shard_rows * head_count
    block_rows = min(512, group_rows)
    seq_count = lax.axis_size("seq")
    own_rows = attn_in.shape[0]
    own_latent = norm_latent.shape[0]
    own_units = down_proj.shape[0]
    units = seq_count * own_units
    padded = -(-units // 128) * 128
    device_count = seq_count * head_count
    proj_cols = attn_in.shape[1]
    gain_cols = jnp.stack(
        [norm_attn, norm_mlp, jnp.pad(norm_latent, (0, own_rows - own_latent))], axis=1
    )
    packed = jnp.concatenate([attn_in, jnp.pad(gain_cols, ((0, 0), (0, 125)))], axis=1)
    pieces = gate_up.reshape(own_rows, 2, seq_count, head_count, own_units)
    pieces = pieces.transpose(3, 1, 0, 2, 4).reshape(head_count, 2, own_rows, units)
    pieces = jnp.pad(pieces, ((0, 0), (0, 0), (0, 0), (0, padded - units)))
    cot_all = lax.all_gather(cotangent, "head", axis=0, tiled=True)
    packed_all, turned = gather_and_swap(packed, pieces, seq_count, head_count, 0)
    weight_gu = lax.all_gather(turned[None], "seq", axis=0, tiled=True)
    weight_down = lax.all_gather(tie(down_proj, turned), "seq", axis=0, tiled=True)
    weight_down = jnp.pad(weight_down, ((0, padded - units), (0, 0)))
    weight_in = packed_all[:, :proj_cols]
    gain_attn = packed_all[:, proj_cols].astype(jnp.float32)
    gain_mlp = packed_all[:, proj_cols + 1].astype(jnp.float32)
    gain_latent = (
        packed_all[:, proj_cols + 2]
        .reshape(device_count, own_rows)[:, :own_latent]
        .reshape(device_count * own_latent)
        .astype(jnp.float32)
    )
    starts = segment_starts(segments[0])
    first_keys = starts[::block_rows] // block_rows
    cosine, sine = angles(starts)
    row_start = head_place * shard_rows
    cos_local = lax.dynamic_slice_in_dim(cosine, row_start, shard_rows, 0)
    sin_local = lax.dynamic_slice_in_dim(sine, row_start, shard_rows, 0)
    inputs_f = inputs.astype(jnp.float32)
    normed = rms_norm(inputs_f, gain_attn).astype(jnp.bfloat16)
    projected = jnp.dot(normed, weight_in, preferred_element_type=jnp.float32)
    latent = projected[:, :QR]
    key_raw = projected[:, QR : QR + DH]
    latent_n = rms_norm(latent, gain_latent).astype(jnp.bfloat16)
    keys_local = rotary(key_raw, cos_local, sin_local).astype(jnp.bfloat16)
    values_local = projected[:, QR + DH :].astype(jnp.bfloat16)
    joined_all = gather_head(
        tie(jnp.concatenate([latent_n, keys_local, values_local], axis=1), cot_all),
        head_count,
        1,
    )
    attn_part, queries, mixed, stats = attention_forward(
        joined_all, starts[:, None], cosine, sine, query_up, out_proj, first_keys, block_rows
    )
    attn_out = reduce_head(attn_part, head_count, 2)
    hidden = inputs_f + attn_out
    normed_mlp = rms_norm(hidden, gain_mlp).astype(jnp.bfloat16)
    nmlp_all = gather_head(tie(normed_mlp, weight_gu, weight_down), head_count, 3)
    nmlp_part, down_part, activated, grad_gate, grad_up = feed_forward(
        nmlp_all, cot_all, weight_gu, weight_down, 256
    )
    grad_nmlp = reduce_head(nmlp_part, head_count, 4)
    gu_part = gu_product(nmlp_all, grad_gate, grad_up, seq_count, 2)
    down_grad = weight_product(
        activated[:, :units],
        cot_all,
        units,
        512,
        (seq_count, own_units, model),
        (seq_count, own_units, 512),
        lambda i, j: (0, 0, j),
    )
    gu_rows = lax.psum_scatter(gu_part, "seq", scatter_dimension=0, tiled=True)
    down_rows = lax.psum_scatter(down_grad, "seq", scatter_dimension=0, tiled=True)
    norm_value, mlp_back = jax.vjp(rms_norm, hidden, gain_mlp)
    grad_hidden_n, mlpnorm_part = mlp_back(grad_nmlp)
    grad_hidden = cotangent.astype(jnp.float32) + grad_hidden_n
    grad_attn = grad_hidden.astype(jnp.bfloat16)
    grad_attn_all = gather_head(tie(grad_attn, gu_part, down_grad), head_count, 5)
    grad_part, grad_query = attention_backward(
        joined_all,
        starts[:, None],
        cosine,
        sine,
        query_up,
        out_proj,
        queries,
        mixed,
        stats,
        grad_attn_all,
        first_keys,
        block_rows,
    )
    head_cols = query_up.shape[1]
    queryup_part = weight_product(
        joined_all,
        grad_query,
        QR // seq_count,
        head_cols,
        (seq_count, QR // seq_count, head_cols),
        (1, QR // seq_count, head_cols),
        lambda i, j: (i, 0, 0),
        height=QR,
    )
    outproj_part = weight_product(
        mixed,
        grad_attn_all,
        head_cols,
        model // seq_count,
        (seq_count, head_cols, model // seq_count),
        (1, head_cols, model // seq_count),
        lambda i, j: (j, 0, 0),
    )
    received = reduce_head(tie(grad_part, queryup_part, outproj_part), head_count, 6)
    received = tie(received, gu_rows, down_rows)
    grad_latent_n, grad_keys, grad_values = (
        received[:, :QR],
        received[:, QR : QR + DH],
        received[:, QR + DH :],
    )
    downproj_grad = down_rows[0].astype(jnp.float32)
    queryup_grad = lax.psum_scatter(queryup_part, "seq", scatter_dimension=0, tiled=True)
    queryup_grad = queryup_grad[0].astype(jnp.float32)
    outproj_grad = lax.psum_scatter(outproj_part, "seq", scatter_dimension=0, tiled=True)
    outproj_grad = outproj_grad[0].astype(jnp.float32)
    latent_value, latent_back = jax.vjp(rms_norm, latent, gain_latent)
    grad_latent, latnorm_part = latent_back(grad_latent_n)
    turned_key, key_back = jax.vjp(lambda key_in: rotary(key_in, cos_local, sin_local), key_raw)
    (grad_key_raw,) = key_back(grad_keys)
    grad_proj = jnp.concatenate([grad_latent, grad_key_raw, grad_values], axis=1).astype(
        jnp.bfloat16
    )
    grad_normed = contract(grad_proj, weight_in)
    input_value, input_back = jax.vjp(rms_norm, inputs_f, gain_attn)
    grad_input_n, attnnorm_part = input_back(grad_normed)
    input_grad = grad_hidden + grad_input_n
    latent_col = jnp.pad(
        latnorm_part.reshape(device_count, own_latent), ((0, 0), (0, own_rows - own_latent))
    ).reshape(device_count * own_rows)
    gain_parts = jnp.stack([attnnorm_part, mlpnorm_part, latent_col], axis=1)
    gain_parts = jnp.pad(gain_parts, ((0, 0), (0, 125))).astype(jnp.bfloat16)
    packed_part = packed_product(normed, grad_proj, gain_parts, min(512, model))
    packed_grad, down_out, gu_back = reduce_and_swap(
        packed_part, down_part, gu_rows[0], seq_count, head_count, 7
    )
    layer_out = (hidden + down_out).astype(jnp.bfloat16)
    gateup_grad = (
        gu_back[..., :units]
        .reshape(head_count, 2, own_rows, seq_count, own_units)
        .transpose(2, 1, 3, 0, 4)
        .reshape(own_rows, 2 * device_count * own_units)
        .astype(jnp.float32)
    )
    attnin_grad = packed_grad[:, :proj_cols]
    attnnorm_grad = packed_grad[:, proj_cols]
    mlpnorm_grad = packed_grad[:, proj_cols + 1]
    latnorm_grad = packed_grad[:own_latent, proj_cols + 2]
    return (
        layer_out,
        input_grad,
        attnnorm_grad,
        attnin_grad,
        latnorm_grad,
        queryup_grad,
        outproj_grad,
        mlpnorm_grad,
        gateup_grad,
        downproj_grad,
    )


def solution(mesh):
    in_specs = (
        P(("seq", "head"), None),
        P("seq", None),
        P(("seq", "head"), None),
        P(("seq", "head")),
        P(("seq", "head"), None),
        P(("seq", "head")),
        P(None, "head"),
        P("head", None),
        P(("seq", "head")),
        P(("seq", "head"), None),
        P(("seq", "head"), None),
    )
    out_specs = (
        P(("seq", "head"), None),
        P(("seq", "head"), None),
        P(("seq", "head")),
        P(("seq", "head"), None),
        P(("seq", "head")),
        P("seq", "head"),
        P("head", "seq"),
        P(("seq", "head")),
        P(("seq", "head"), None),
        P(("seq", "head"), None),
    )
    return jax.shard_map(shards, mesh=mesh, in_specs=in_specs, out_specs=out_specs, check_vma=False)
```
